768 devices in a mesh: wide: 192 (over z, y, x_lo), narrow: 4 (over x_hi, core).
Axes of the slice: x: 4 (x_hi: 2, x_lo: 2; x = x_hi * 2 + x_lo), y: 8, z: 12, core: 2. Of those that a mesh axis runs over, the one named last changes fastest.
Arguments:
- child_spec: bfloat16 [192, 32, 2, 2, 2048], P('wide', 'narrow'), may hold values from -6 to 6
- interp_theta: bfloat16 [64, 32], replicated, may hold values from -1 to 1
- interp_phi: bfloat16 [128, 64], replicated, may hold values from -0.75 to 0.75
- shift_angle: float32 [8, 8192], replicated, may hold values from -3.140625 to 3.140625
- trans_op: float32 [32, 2, 8192], replicated, may hold values from -0.6 to 0.6
- parent_of: int32 [192, 32], P('wide', 'narrow'), may hold values from 0 to 3, as said below
- octant_of: int32 [192, 32], P('wide', 'narrow'), may hold values from 0 to 7, as said below
- sources: int32 [192, 4, 6], P('wide'), may hold values from 0 to 11, as said below
- kinds: int32 [192, 4, 6], P('wide'), may hold values from 0 to 31
Outputs:
- child_incoming: float32 [192, 32, 2, 2, 2048], P('wide', 'narrow')
The draws below stay inside these ranges and needn't reach their ends.
Inputs may be any that keep to these rules, and one draw needn't show every extreme that they name: `parent_of`: in every layer each parent has exactly 8 children, spread over the layer's children by a random permutation. `octant_of`: the 8 children of a parent have the octants 0 to 7 once each. `sources`: entry j of a list names a parent of layer offset j // 2 - 1, as that offset plus one times 4 plus the parent's index in its layer.
All inputs are finite; a program needn't handle non-finite values.
Results may differ from the reference program's by a relative error of at most 0.015.
Values may be sent and summed in bfloat16 or wider, within the bound.
A program may use at most 32 MiB of HBM per device.

```python
import jax
import jax.numpy as jnp
from jax import lax

TC = 32
PC = 64
TP = 64
PP = 128
INC = 2
NB = 6
NT = 32
NL = 192
CHL = 32
PAR_L = 4
N_NARROW = 4


def octree_slots(key):
    base_key = jax.random.fold_in(key, 7)
    layer_keys = jax.random.split(base_key, NL)
    return jax.vmap(lambda layer_key: jax.random.permutation(layer_key, CHL))(layer_keys).astype(jnp.int32)


def draw_parent_of(key, part):
    return octree_slots(key) // 8


def draw_octant_of(key, part):
    return octree_slots(key) % 8


def draw_sources(key, part):
    chosen = jax.random.randint(jax.random.fold_in(key, 11), (NL, PAR_L, NB), 0, PAR_L).astype(jnp.int32)
    chosen = chosen.at[:, 0, 0].set(0)
    chosen = chosen.at[:, PAR_L - 1, NB - 1].set(PAR_L - 1)
    offsets = (jnp.arange(NB, dtype=jnp.int32) // (NB // 3))[None, None, :]
    return offsets * PAR_L + chosen


def with_ends(result, own_key, smallest, top_value):
    shape = result.shape
    spot = [jax.random.randint(jax.random.fold_in(own_key, axis), (), 0, shape[axis]) for axis in range(len(shape))]
    result = result.at[tuple(spot)].set(smallest)
    longest = shape.index(max(shape))
    spot[longest] = (spot[longest] + 1) % shape[longest]
    return result.at[tuple(spot)].set(top_value)


def block_levels(key, shape, shards, smallest, top_value):
    level, own = 1.0, jax.random.fold_in(key, 6)
    for dim, shards_of in shards:
        heights = jnp.exp(jax.random.uniform(jax.random.fold_in(own, dim), (shards_of,), jnp.float32, smallest / len(shards), top_value / len(shards)))
        level = level * jnp.repeat(heights, shape[dim] // shards_of).reshape([-1 if axis == dim else 1 for axis in range(len(shape))])
    return level


def scatter_about(rng, extent, width, reach, cuts=(), held_as=jnp.bfloat16):
    factor_of = block_levels(rng, extent, cuts, -0.22, 0.18) if cuts else 1.0
    drawn = jax.random.normal(rng, extent, jnp.float32) * width * factor_of
    return jnp.minimum(jnp.maximum(drawn, -reach), reach).astype(held_as)


def setup_inputs(seed: int = 0) -> dict:
    key_of = jax.random.split(jax.random.key(seed), 10)
    return {
        "child_spec": scatter_about(key_of[0], (NL, CHL, 2, INC, TC * PC), 1.0, 6.0, ((0, 192), (1, 4))),
        "interp_theta": scatter_about(key_of[1], (TP, TC), TC ** -0.5, 1.0),
        "interp_phi": scatter_about(key_of[2], (PP, PC), PC ** -0.5, 0.75),
        "shift_angle": jnp.clip(jax.random.uniform(key_of[3], (8, TP * PP), jnp.float32, -3.140625, 3.140625), -3.140625, 3.140625),
        "trans_op": scatter_about(key_of[4], (NT, 2, TP * PP), 0.1, 0.6, (), jnp.float32),
        "parent_of": draw_parent_of(jax.random.fold_in(key_of[9], 71), 0),
        "octant_of": draw_octant_of(jax.random.fold_in(key_of[9], 71), 0),
        "sources": draw_sources(jax.random.fold_in(key_of[9], 71), 0),
        "kinds": with_ends(jax.random.randint(key_of[8], (NL, PAR_L, NB), 0, NT), jax.random.fold_in(key_of[8], 1), 0, NT - 1).astype(jnp.int32),
    }


def rounded(values):
    return lax.optimization_barrier(values.astype(jnp.bfloat16)).astype(jnp.float32)


def translate(pooled, source_ids, kind_ids, table):
    real_sum = jnp.zeros((source_ids.shape[0],) + pooled.shape[2:], jnp.float32)
    imag_sum = jnp.zeros((source_ids.shape[0],) + pooled.shape[2:], jnp.float32)
    for column in range(source_ids.shape[1]):
        picked = jnp.take(pooled, source_ids[:, column], axis=0).astype(jnp.float32)
        chosen = jnp.take(table, kind_ids[:, column], axis=0)
        table_real = chosen[:, 0][:, None, :]
        table_imag = chosen[:, 1][:, None, :]
        real_sum = real_sum + table_real * picked[:, 0] - table_imag * picked[:, 1]
        imag_sum = imag_sum + table_real * picked[:, 1] + table_imag * picked[:, 0]
    return jnp.stack([real_sum, imag_sum], 1).astype(jnp.bfloat16)


def reference(child_spec, interp_theta, interp_phi, shift_angle, trans_op, parent_of, octant_of, sources, kinds):
    highest = lax.Precision.HIGHEST
    theta_mat = interp_theta.astype(jnp.float32)
    phi_mat = interp_phi.astype(jnp.float32)
    cosine_tab = jnp.cos(shift_angle)
    sine_tab = jnp.sin(shift_angle)
    parent_ids = jnp.arange(PAR_L, dtype=jnp.int32)
    group_len = CHL // N_NARROW

    def aggregate(layer_item):
        spectra, parent_row, octant_row = layer_item
        child_grid = spectra.astype(jnp.float32).reshape(CHL, 2, INC, TC, PC)
        coarse = rounded(jnp.einsum("ctiap,ha->ctihp", child_grid, theta_mat, precision=highest))
        fine = jnp.einsum("ctihp,qp->ctihq", coarse, phi_mat, precision=highest).reshape(CHL, 2, INC, TP * PP)
        cosine_row = cosine_tab[octant_row][:, None, :]
        sine_row = sine_tab[octant_row][:, None, :]
        real_part = fine[:, 0] * cosine_row - fine[:, 1] * sine_row
        imag_part = fine[:, 0] * sine_row + fine[:, 1] * cosine_row
        shifted = jnp.stack([real_part, imag_part], 1).reshape(N_NARROW, group_len, 2, INC, TP * PP)
        select_hot = (parent_row[None, :] == parent_ids[:, None]).astype(jnp.float32)
        select_hot = select_hot.reshape(PAR_L, N_NARROW, group_len)
        partial_value = jnp.einsum("pgc,gctid->gptid", select_hot, shifted, precision=highest)
        partial_value = rounded(partial_value)
        return jnp.sum(partial_value, 0).astype(jnp.bfloat16)

    parents = lax.map(aggregate, (child_spec, parent_of, octant_of))
    zero_layer = jnp.zeros((1, PAR_L, 2, INC, TP * PP), jnp.bfloat16)
    padded = jnp.concatenate([zero_layer, parents, zero_layer], 0)

    def disaggregate(layer_item):
        layer_index, parent_row, octant_row, source_row, kind_row = layer_item
        pooled = lax.dynamic_slice_in_dim(padded, layer_index, 3, 0).reshape(3 * PAR_L, 2, INC, TP * PP)
        incoming = translate(pooled, source_row, kind_row, trans_op)
        picked = incoming[parent_row].astype(jnp.float32)
        cosine_row = cosine_tab[octant_row][:, None, :]
        sine_row = sine_tab[octant_row][:, None, :]
        real_part = picked[:, 0] * cosine_row + picked[:, 1] * sine_row
        imag_part = picked[:, 1] * cosine_row - picked[:, 0] * sine_row
        back = rounded(jnp.stack([real_part, imag_part], 1)).reshape(CHL, 2, INC, TP, PP)
        half = rounded(jnp.einsum("ctihq,qp->ctihp", back, phi_mat, precision=highest))
        result_field = jnp.einsum("ctihp,ha->ctiap", half, theta_mat, precision=highest)
        return result_field.reshape(CHL, 2, INC, TC * PC)

    layer_ids = jnp.arange(NL, dtype=jnp.int32)
    return lax.map(disaggregate, (layer_ids, parent_of, octant_of, sources, kinds))
```

```python
import functools

import jax
import jax.numpy as jnp
from jax import lax
from jax.experimental import pallas as pl
from jax.experimental.pallas import tpu as pltpu
from jax.sharding import PartitionSpec as P

MESH = pl.DeviceIdType.MESH
F32 = jnp.float32
BF16 = jnp.bfloat16


def iota(shape, dim):
    return lax.broadcasted_iota(jnp.int32, shape, dim)


def one_hot(mask):
    return jnp.where(mask, 1.0, 0.0).astype(BF16)


def dot(a, b, dims=((1,), (0,))):
    return lax.dot_general(a, b, (dims, ((), ())), preferred_element_type=F32)


def polar_matrices(theta_t):
    row = iota((128, 32), 0)
    pick_row = one_hot(iota((128, 32), 1) == 2 * ((row >> 1) & 15) + (row >> 6))
    spread = one_hot((iota((64, 256), 1) & 63) == iota((64, 256), 0))
    short = dot(pick_row, theta_t).astype(BF16)
    full = dot(short, spread)
    row, col = iota((128, 256), 0), iota((128, 256), 1)
    same = ((col >> 7) == ((row >> 5) & 1)) & (((col >> 6) & 1) == (row & 1))
    down = jnp.where(same, full, 0.0).astype(BF16)
    col = iota((32, 128), 1)
    pick_col = one_hot(iota((32, 128), 0) == 2 * ((col >> 1) & 15) + (col >> 6))
    spread = one_hot((iota((256, 64), 0) & 63) == iota((256, 64), 1))
    short = dot(theta_t, pick_col, ((0,), (0,))).astype(BF16)
    full = dot(spread, short)
    row, col = iota((256, 128), 0), iota((256, 128), 1)
    same = ((row >> 7) == ((col >> 5) & 1)) & (((row >> 6) & 1) == (col & 1))
    up = jnp.where(same, full, 0.0).astype(BF16)
    return up, down


def azimuth_up(phi_t):
    full = phi_t.astype(F32)
    full = jnp.concatenate([full, full], axis=1)
    full = jnp.concatenate([full, full], axis=0)
    same = (iota((128, 256), 0) >> 6) == (iota((128, 256), 1) >> 7)
    return jnp.where(same, full, 0.0).astype(BF16)


def azimuth_down(phi_t):
    spread = one_hot((iota((64, 128), 1) & 63) == iota((64, 128), 0))
    full = dot(phi_t, spread, ((0,), (0,)))
    full = jnp.concatenate([full, full], axis=0)
    same = (iota((256, 128), 0) >> 7) == (iota((256, 128), 1) >> 6)
    return jnp.where(same, full, 0.0).astype(BF16)


def kernel(
    layers,
    parent_ref,
    octant_ref,
    source_ref,
    kind_ref,
    spec_ref,
    theta_ref,
    phi_ref,
    angle_ref,
    trans_hbm,
    out_ref,
    table,
    cos_tab,
    sin_tab,
    stacked,
    fine,
    part,
    pair_in,
    chip_out,
    chip_own,
    chip_in,
    own,
    below,
    above,
    trans_raw,
    trans,
    field,
    inc_own,
    inc_chip,
    inc_pair,
    inc_far,
    back,
    sides,
    load_sem,
    send_sem,
    recv_sem,
):
    wide = lax.axis_index("wide")
    narrow = lax.axis_index("narrow")
    chip = narrow // 2
    core = narrow % 2
    pair_id = {"wide": wide, "narrow": 2 * chip + (1 - core)}
    chip_id = {"wide": wide, "narrow": 2 * (1 - chip) + core}
    up_id = {"wide": lax.rem(wide + 1, layers), "narrow": narrow}
    down_id = {"wide": lax.rem(wide + layers - 1, layers), "narrow": narrow}

    barrier = pltpu.get_barrier_semaphore()
    for target in (pair_id, chip_id, up_id, down_id):
        pl.semaphore_signal(barrier, inc=1, device_id=target, device_id_type=MESH)

    quarter = 2 * core + chip
    load = pltpu.make_async_copy(
        trans_hbm.at[:, pl.ds(pl.multiple_of(quarter * 32, 32), 32), :], trans_raw, load_sem
    )
    load.start()

    def remote(slot, src, dst, target):
        return pltpu.make_async_remote_copy(
            src_ref=src,
            dst_ref=dst,
            send_sem=send_sem.at[slot],
            recv_sem=recv_sem.at[slot],
            device_id=target,
            device_id_type=MESH,
        )

    for wave, tab in ((jnp.cos, cos_tab), (jnp.sin, sin_tab)):
        table[...] = wave(angle_ref[...])
        for octant in range(8):
            tab[octant] = table[pl.ds(octant, 64, stride=8), :]

    polar_up, polar_down = polar_matrices(theta_ref[...])
    phi_t = phi_ref[...]
    coarse = dot(spec_ref[...], azimuth_up(phi_t)).astype(BF16)
    for child in range(8):
        for e in range(2):
            stacked[e * 64 : e * 64 + 64, child * 128 : child * 128 + 128] = coarse[
                child * 64 : child * 64 + 64, e * 128 : e * 128 + 128
            ]
    raised = dot(polar_up, stacked[...])
    for child in range(8):
        fine[child] = raised[:, child * 128 : child * 128 + 128]

    def partials(which):
        rows = pl.ds(pl.multiple_of(which * 16, 16), 16)
        for i in range(2):

            def add(child, sums):
                octant = octant_ref[0, child]
                mine = parent_ref[0, child]
                real = fine[child, pl.ds(pl.multiple_of(i * 64 + which * 16, 16), 16), :]
                imag = fine[child, pl.ds(pl.multiple_of(128 + i * 64 + which * 16, 16), 16), :]
                cosine = cos_tab[octant, rows, :]
                sine = sin_tab[octant, rows, :]
                turned_real = real * cosine - imag * sine
                turned_imag = real * sine + imag * cosine
                new = []
                for parent in range(4):
                    weight = jnp.where(mine == parent, 1.0, 0.0)
                    new.append(sums[2 * parent] + weight * turned_real)
                    new.append(sums[2 * parent + 1] + weight * turned_imag)
                return tuple(new)

            sums = lax.fori_loop(0, 8, add, tuple(jnp.zeros((16, 128), F32) for _ in range(8)))
            for parent in range(4):
                part[which, parent, 0, i] = sums[2 * parent].astype(BF16)
                part[which, parent, 1, i] = sums[2 * parent + 1].astype(BF16)

    away = 2 * (1 - core)
    partials(away)
    partials(away + 1)
    pl.semaphore_wait(barrier, 4)
    to_pair = remote(0, part.at[pl.ds(away, 2)], pair_in, pair_id)
    to_pair.start()
    partials(2 * core)
    partials(2 * core + 1)
    to_pair.wait_recv()

    other = 2 * core + (1 - chip)
    chip_out[...] = (part[other].astype(F32) + pair_in[1 - chip].astype(F32)).astype(BF16)
    to_chip = remote(1, chip_out, chip_in, chip_id)
    to_chip.start()
    chip_own[...] = part[quarter].astype(F32) + pair_in[chip].astype(F32)

    load.wait()

    def split(kind, carry):
        for t in range(2):
            trans[kind, t] = trans_raw[kind, pl.ds(t, 16, stride=2), :]
        return carry

    lax.fori_loop(0, 32, split, 0)

    to_chip.wait_recv()
    own[...] = (chip_own[...] + chip_in[...].astype(F32)).astype(BF16)
    to_up = remote(2, own, below, up_id)
    to_down = remote(3, own, above, down_id)
    to_up.start()
    to_down.start()

    def translate(columns, pool, start):
        def one(parent, carry):
            if start:
                sums = [jnp.zeros((16, 128), F32) for _ in range(4)]
            else:
                sums = [field[parent, t, i] for t in range(2) for i in range(2)]
            for column in columns:
                source = lax.rem(source_ref[0, parent, column], 4)
                kind = kind_ref[0, parent, column]
                table_real = trans[kind, 0]
                table_imag = trans[kind, 1]
                for i in range(2):
                    real = pool[source, 0, i].astype(F32)
                    imag = pool[source, 1, i].astype(F32)
                    sums[i] = sums[i] + table_real * real - table_imag * imag
                    sums[2 + i] = sums[2 + i] + table_real * imag + table_imag * real
            for t in range(2):
                for i in range(2):
                    field[parent, t, i] = sums[2 * t + i]
            return carry

        lax.fori_loop(0, 4, one, 0)

    translate((2, 3), own, True)
    to_up.wait_recv()

    @pl.when(wide == 0)
    def _():
        below[...] = jnp.zeros_like(below)

    translate((0, 1), below, False)
    to_down.wait_recv()

    @pl.when(wide == layers - 1)
    def _():
        above[...] = jnp.zeros_like(above)

    translate((4, 5), above, False)
    inc_own[...] = field[...].astype(BF16)

    inc_to_chip = remote(4, inc_own, inc_chip, chip_id)
    inc_to_pair = remote(5, inc_own, inc_pair, pair_id)
    inc_to_chip.start()
    inc_to_pair.start()

    def turn_back(values, which):
        rows = pl.ds(pl.multiple_of(which * 16, 16), 16)

        def one(child, carry):
            parent = parent_ref[0, child]
            octant = octant_ref[0, child]
            cosine = cos_tab[octant, rows, :]
            sine = sin_tab[octant, rows, :]
            for i in range(2):
                real = values[parent, 0, i].astype(F32)
                imag = values[parent, 1, i].astype(F32)
                back[child, pl.ds(pl.multiple_of(i * 64 + which * 16, 16), 16), :] = (
                    real * cosine + imag * sine
                ).astype(BF16)
                back[child, pl.ds(pl.multiple_of(128 + i * 64 + which * 16, 16), 16), :] = (
                    imag * cosine - real * sine
                ).astype(BF16)
            return carry

        lax.fori_loop(0, 8, one, 0)

    turn_back(inc_own, quarter)
    inc_to_pair.wait_recv()
    turn_back(inc_pair, 2 * (1 - core) + chip)
    inc_to_chip.wait_recv()
    inc_forward = remote(6, inc_chip, inc_far, pair_id)
    inc_forward.start()
    turn_back(inc_chip, other)
    inc_forward.wait_recv()
    turn_back(inc_far, 2 * (1 - core) + (1 - chip))

    down = azimuth_down(phi_t)
    for child in range(8):
        lowered = dot(polar_down, back[child]).astype(BF16)
        for e in range(2):
            sides[child * 64 : child * 64 + 64, e * 128 : e * 128 + 128] = lowered[
                e * 64 : e * 64 + 64, :
            ]
    out_ref[...] = dot(sides[...], down)

    for copy in (to_pair, to_chip, to_up, to_down, inc_to_chip, inc_to_pair, inc_forward):
        copy.wait_send()


def body(
    child_spec,
    interp_theta,
    interp_phi,
    shift_angle,
    trans_op,
    parent_of,
    octant_of,
    sources,
    kinds,
):
    layers = lax.axis_size("wide")
    rows = child_spec.reshape(8, 2, 2, 16, 128).transpose(0, 1, 3, 2, 4).reshape(512, 128)
    angle = shift_angle.reshape(8, 64, 128).transpose(1, 0, 2).reshape(512, 128)
    planes = trans_op.reshape(32, 2, 64, 128).transpose(0, 2, 1, 3).reshape(32, 128, 128)
    quarter = (4, 2, 2, 16, 128)
    vmem = pl.BlockSpec(memory_space=pltpu.VMEM)
    smem = pl.BlockSpec(memory_space=pltpu.SMEM)
    result = pl.pallas_call(
        functools.partial(kernel, layers),
        out_shape=jax.ShapeDtypeStruct((512, 128), F32),
        in_specs=[smem] * 4 + [vmem] * 4 + [pl.BlockSpec(memory_space=pl.ANY)],
        out_specs=vmem,
        scratch_shapes=[
            pltpu.VMEM((512, 128), F32),
            pltpu.VMEM((8, 64, 128), F32),
            pltpu.VMEM((8, 64, 128), F32),
            pltpu.VMEM((128, 1024), BF16),
            pltpu.VMEM((8, 256, 128), F32),
            pltpu.VMEM((4,) + quarter, BF16),
            pltpu.VMEM((2,) + quarter, BF16),
            pltpu.VMEM(quarter, BF16),
            pltpu.VMEM(quarter, F32),
            pltpu.VMEM(quarter, BF16),
            pltpu.VMEM(quarter, BF16),
            pltpu.VMEM(quarter, BF16),
            pltpu.VMEM(quarter, BF16),
            pltpu.VMEM((32, 32, 128), F32),
            pltpu.VMEM((32, 2, 16, 128), F32),
            pltpu.VMEM(quarter, F32),
            pltpu.VMEM(quarter, BF16),
            pltpu.VMEM(quarter, BF16),
            pltpu.VMEM(quarter, BF16),
            pltpu.VMEM(quarter, BF16),
            pltpu.VMEM((8, 256, 128), BF16),
            pltpu.VMEM((512, 256), BF16),
            pltpu.SemaphoreType.DMA,
            pltpu.SemaphoreType.DMA((7,)),
            pltpu.SemaphoreType.DMA((7,)),
        ],
        compiler_params=pltpu.CompilerParams(collective_id=0, has_side_effects=True),
        name="mlfma",
    )(parent_of, octant_of, sources, kinds, rows, interp_theta.T, interp_phi.T, angle, planes)
    result = result.reshape(8, 2, 16, 2, 128).transpose(0, 1, 3, 2, 4)
    return result.reshape(1, 8, 2, 2, 2048)


def solution(mesh):
    placed = (
        P("wide", "narrow", None, None, None),
        P(),
        P(),
        P(),
        P(),
        P("wide", "narrow"),
        P("wide", "narrow"),
        P("wide", None, None),
        P("wide", None, None),
    )
    return jax.shard_map(
        body,
        mesh=mesh,
        in_specs=placed,
        out_specs=P("wide", "narrow", None, None, None),
        check_vma=False,
    )
```

```python
import functools

import jax
import jax.numpy as jnp
from jax import lax
from jax.experimental import pallas as pl
from jax.experimental.pallas import tpu as pltpu
from jax.sharding import PartitionSpec as P

MESH = pl.DeviceIdType.MESH
F32 = jnp.float32
BF16 = jnp.bfloat16


def iota(shape, dim):
    return lax.broadcasted_iota(jnp.int32, shape, dim)


def one_hot(mask):
    return jnp.where(mask, 1.0, 0.0).astype(BF16)


def dot(a, b, dims=((1,), (0,))):
    return lax.dot_general(a, b, (dims, ((), ())), preferred_element_type=F32)


def polar_matrices(theta_t):
    row = iota((128, 32), 0)
    pick_row = one_hot(iota((128, 32), 1) == 2 * ((row >> 1) & 15) + (row >> 6))
    spread = one_hot((iota((64, 256), 1) & 63) == iota((64, 256), 0))
    short = dot(pick_row, theta_t).astype(BF16)
    full = dot(short, spread)
    row, col = iota((128, 256), 0), iota((128, 256), 1)
    same = ((col >> 7) == ((row >> 5) & 1)) & (((col >> 6) & 1) == (row & 1))
    down = jnp.where(same, full, 0.0).astype(BF16)
    col = iota((32, 128), 1)
    pick_col = one_hot(iota((32, 128), 0) == 2 * ((col >> 1) & 15) + (col >> 6))
    spread = one_hot((iota((256, 64), 0) & 63) == iota((256, 64), 1))
    short = dot(theta_t, pick_col, ((0,), (0,))).astype(BF16)
    full = dot(spread, short)
    row, col = iota((256, 128), 0), iota((256, 128), 1)
    same = ((row >> 7) == ((col >> 5) & 1)) & (((row >> 6) & 1) == (col & 1))
    up = jnp.where(same, full, 0.0).astype(BF16)
    return up, down


def azimuth_up(phi_t):
    full = phi_t.astype(F32)
    full = jnp.concatenate([full, full], axis=1)
    full = jnp.concatenate([full, full], axis=0)
    same = (iota((128, 256), 0) >> 6) == (iota((128, 256), 1) >> 7)
    return jnp.where(same, full, 0.0).astype(BF16)


def azimuth_down(phi_t):
    spread = one_hot((iota((64, 128), 1) & 63) == iota((64, 128), 0))
    full = dot(phi_t, spread, ((0,), (0,)))
    full = jnp.concatenate([full, full], axis=0)
    same = (iota((256, 128), 0) >> 7) == (iota((256, 128), 1) >> 6)
    return jnp.where(same, full, 0.0).astype(BF16)


def cos_sin(angle):
    half = 0.5 * angle
    z = half * half
    sine, cosine = 1.0 / 6227020800.0, 1.0 / 479001600.0
    for below_sine, below_cosine in (
        (-1.0 / 39916800.0, -1.0 / 3628800.0),
        (1.0 / 362880.0, 1.0 / 40320.0),
        (-1.0 / 5040.0, -1.0 / 720.0),
        (1.0 / 120.0, 1.0 / 24.0),
        (-1.0 / 6.0, -0.5),
        (1.0, 1.0),
    ):
        sine = sine * z + below_sine
        cosine = cosine * z + below_cosine
    sine = sine * half
    twice = sine + sine
    return 1.0 - twice * sine, twice * cosine


def kernel(
    layers,
    parent_ref,
    octant_ref,
    source_ref,
    kind_ref,
    spec_ref,
    theta_ref,
    phi_ref,
    angle_ref,
    trans_hbm,
    out_ref,
    cos_rows,
    sin_rows,
    cos_tab,
    sin_tab,
    stacked,
    fine,
    part,
    pair_in,
    chip_out,
    chip_own,
    chip_in,
    own,
    below_0,
    below_1,
    above_0,
    above_1,
    trans_raw,
    trans,
    field,
    inc_own,
    inc_chip_0,
    inc_chip_1,
    inc_pair_0,
    inc_pair_1,
    inc_far_0,
    inc_far_1,
    back,
    sides,
    load_sem,
    send_sem,
    recv_sem,
):
    below, above = (below_0, below_1), (above_0, above_1)
    inc_chip, inc_pair, inc_far = (inc_chip_0, inc_chip_1), (inc_pair_0, inc_pair_1), (inc_far_0, inc_far_1)
    wide = lax.axis_index("wide")
    narrow = lax.axis_index("narrow")
    chip = narrow // 2
    core = narrow % 2
    odd = wide % 2
    turn = (wide // 2) % 2
    mine = (chip + turn) % 2
    theirs = 1 - mine
    pair_id = {"wide": wide, "narrow": 2 * chip + (1 - core)}
    chip_id = {"wide": wide, "narrow": 2 * (1 - chip) + core}
    up_id = {"wide": lax.rem(wide + 1, layers), "narrow": 2 * ((chip + odd) % 2) + core}
    down_id = {
        "wide": lax.rem(wide + layers - 1, layers),
        "narrow": 2 * ((chip + 1 - odd) % 2) + core,
    }
    has_up = wide < layers - 1
    has_down = wide > 0

    def greet(target):
        pl.semaphore_signal(barrier, inc=1, device_id=target, device_id_type=MESH)

    barrier = pltpu.get_barrier_semaphore()
    greet(pair_id)
    greet(chip_id)

    @pl.when(has_up)
    def _():
        greet(up_id)

    @pl.when(has_down)
    def _():
        greet(down_id)

    quarter = 2 * core + mine
    load = pltpu.make_async_copy(
        trans_hbm.at[:, pl.ds(pl.multiple_of(quarter * 32, 32), 32), :], trans_raw, load_sem
    )
    load.start()

    def remote(slot, src, dst, target):
        return pltpu.make_async_remote_copy(
            src_ref=src,
            dst_ref=dst,
            send_sem=send_sem.at[slot],
            recv_sem=recv_sem.at[slot],
            device_id=target,
            device_id_type=MESH,
        )

    away = 2 * (1 - core)
    to_pair = [remote(i, part.at[i, pl.ds(away, 2)], pair_in.at[i], pair_id) for i in range(2)]
    to_chip = [remote(2 + i, chip_out.at[i], chip_in.at[i], chip_id) for i in range(2)]
    to_up = [remote(4 + i, own.at[i], below[i], up_id) for i in range(2)]
    to_down = [remote(6 + i, own.at[i], above[i], down_id) for i in range(2)]
    inc_to_chip = [remote(8 + i, inc_own.at[i], inc_chip[i], chip_id) for i in range(2)]
    inc_to_pair = [remote(10 + i, inc_own.at[i], inc_pair[i], pair_id) for i in range(2)]
    inc_forward = [remote(12 + i, inc_chip[i], inc_far[i], pair_id) for i in range(2)]

    cos_rows[...], sin_rows[...] = cos_sin(angle_ref[...])
    for rows_of, tab in ((cos_rows, cos_tab), (sin_rows, sin_tab)):
        for octant in range(8):
            tab[octant] = rows_of[pl.ds(octant, 64, stride=8), :]

    polar_up, polar_down = polar_matrices(theta_ref[...])
    phi_t = phi_ref[...]
    coarse = dot(spec_ref[...], azimuth_up(phi_t)).astype(BF16)
    for child in range(8):
        for e in range(2):
            stacked[e * 64 : e * 64 + 64, child * 128 : child * 128 + 128] = coarse[
                child * 64 : child * 64 + 64, e * 128 : e * 128 + 128
            ]
    raised = dot(polar_up, stacked[...])
    for child in range(8):
        fine[child] = raised[:, child * 128 : child * 128 + 128]

    def partials(i, which):
        rows = pl.ds(pl.multiple_of(which * 16, 16), 16)

        def add(step, sums):
            sums = list(sums)
            for child in (2 * step, 2 * step + 1):
                octant = octant_ref[0, child]
                home = parent_ref[0, child]
                real = fine[child, pl.ds(pl.multiple_of(i * 64 + which * 16, 16), 16), :]
                imag = fine[child, pl.ds(pl.multiple_of(128 + i * 64 + which * 16, 16), 16), :]
                cosine = cos_tab[octant, rows, :]
                sine = sin_tab[octant, rows, :]
                turned_real = real * cosine - imag * sine
                turned_imag = real * sine + imag * cosine
                for parent in range(4):
                    weight = jnp.where(home == parent, 1.0, 0.0)
                    sums[2 * parent] = sums[2 * parent] + weight * turned_real
                    sums[2 * parent + 1] = sums[2 * parent + 1] + weight * turned_imag
            return tuple(sums)

        sums = lax.fori_loop(0, 4, add, tuple(jnp.zeros((16, 128), F32) for _ in range(8)))
        for parent in range(4):
            part[i, which, parent, 0] = sums[2 * parent].astype(BF16)
            part[i, which, parent, 1] = sums[2 * parent + 1].astype(BF16)

    def over_pair(i):
        to_pair[i].wait_recv()
        gone = part[i, 2 * core + theirs].astype(F32) + pair_in[i, theirs].astype(F32)
        chip_out[i] = gone.astype(BF16)
        to_chip[i].start()
        chip_own[i] = part[i, quarter].astype(F32) + pair_in[i, mine].astype(F32)

    partials(0, away)
    partials(0, away + 1)
    pl.semaphore_wait(barrier, 2 + has_up.astype(jnp.int32) + has_down.astype(jnp.int32))
    to_pair[0].start()
    partials(1, away)
    partials(1, away + 1)
    to_pair[1].start()
    partials(0, 2 * core)
    partials(0, 2 * core + 1)
    over_pair(0)
    partials(1, 2 * core)
    partials(1, 2 * core + 1)
    over_pair(1)

    load.wait()

    def split(kind, carry):
        for t in range(2):
            trans[kind, t] = trans_raw[kind, pl.ds(t, 16, stride=2), :]
        return carry

    lax.fori_loop(0, 32, split, 0)
    down = azimuth_down(phi_t)

    @pl.when(wide == 0)
    def _():
        for ref in below:
            ref[...] = jnp.zeros_like(ref)

    @pl.when(wide == layers - 1)
    def _():
        for ref in above:
            ref[...] = jnp.zeros_like(ref)

    for i in range(2):
        to_chip[i].wait_recv()
        own[i] = (chip_own[i] + chip_in[i].astype(F32)).astype(BF16)

        @pl.when(has_up)
        def _():
            to_up[i].start()

        @pl.when(has_down)
        def _():
            to_down[i].start()

    def translate(i, sources, start):
        def one(parent, carry):
            if start:
                sums = [jnp.zeros((16, 128), F32) for _ in range(2)]
            else:
                sums = [field[i, parent, t] for t in range(2)]
            for column, pool in sources:
                source = lax.rem(source_ref[0, parent, column], 4)
                kind = kind_ref[0, parent, column]
                table_real = trans[kind, 0]
                table_imag = trans[kind, 1]
                real = pool[source, 0].astype(F32)
                imag = pool[source, 1].astype(F32)
                sums[0] = sums[0] + table_real * real - table_imag * imag
                sums[1] = sums[1] + table_real * imag + table_imag * real
            for t in range(2):
                if start:
                    field[i, parent, t] = sums[t]
                else:
                    inc_own[i, parent, t] = sums[t].astype(BF16)
            return carry

        lax.fori_loop(0, 4, one, 0)

    translate(0, ((2, own.at[0]), (3, own.at[0])), True)
    translate(1, ((2, own.at[1]), (3, own.at[1])), True)

    for i in range(2):

        @pl.when(has_down)
        def _():
            to_up[i].wait_recv()

        @pl.when(has_up)
        def _():
            to_down[i].wait_recv()

        translate(i, ((0, below[i]), (1, below[i]), (4, above[i]), (5, above[i])), False)
        inc_to_chip[i].start()
        inc_to_pair[i].start()

    def turn_back(i, values, which):
        rows = pl.ds(pl.multiple_of(which * 16, 16), 16)

        def one(step, carry):
            for child in (2 * step, 2 * step + 1):
                home = parent_ref[0, child]
                octant = octant_ref[0, child]
                cosine = cos_tab[octant, rows, :]
                sine = sin_tab[octant, rows, :]
                real = values[home, 0].astype(F32)
                imag = values[home, 1].astype(F32)
                back[child, pl.ds(pl.multiple_of(i * 64 + which * 16, 16), 16), :] = (
                    real * cosine + imag * sine
                ).astype(BF16)
                back[child, pl.ds(pl.multiple_of(128 + i * 64 + which * 16, 16), 16), :] = (
                    imag * cosine - real * sine
                ).astype(BF16)
            return carry

        lax.fori_loop(0, 4, one, 0)

    for i in range(2):
        turn_back(i, inc_own.at[i], quarter)
    for i in range(2):
        inc_to_pair[i].wait_recv()
        turn_back(i, inc_pair[i], away + mine)
    for i in range(2):
        inc_to_chip[i].wait_recv()
        inc_forward[i].start()
        turn_back(i, inc_chip[i], 2 * core + theirs)
    for i in range(2):
        inc_forward[i].wait_recv()
        turn_back(i, inc_far[i], away + theirs)

    for child in range(8):
        lowered = dot(polar_down, back[child]).astype(BF16)
        for e in range(2):
            sides[child * 64 : child * 64 + 64, e * 128 : e * 128 + 128] = lowered[
                e * 64 : e * 64 + 64, :
            ]
    out_ref[...] = dot(sides[...], down)

    for i in range(2):
        for copies in (to_pair, to_chip, inc_to_chip, inc_to_pair, inc_forward):
            copies[i].wait_send()

        @pl.when(has_up)
        def _():
            to_up[i].wait_send()

        @pl.when(has_down)
        def _():
            to_down[i].wait_send()


def body(
    child_spec,
    interp_theta,
    interp_phi,
    shift_angle,
    trans_op,
    parent_of,
    octant_of,
    sources,
    kinds,
):
    layers = lax.axis_size("wide")
    rows = child_spec.reshape(8, 2, 2, 16, 128).transpose(0, 1, 3, 2, 4).reshape(512, 128)
    angle = shift_angle.reshape(8, 64, 128).transpose(1, 0, 2).reshape(512, 128)
    planes = trans_op.reshape(32, 2, 64, 128).transpose(0, 2, 1, 3).reshape(32, 128, 128)
    quarter = (4, 2, 16, 128)
    vmem = pl.BlockSpec(memory_space=pltpu.VMEM)
    smem = pl.BlockSpec(memory_space=pltpu.SMEM)
    result = pl.pallas_call(
        functools.partial(kernel, layers),
        out_shape=jax.ShapeDtypeStruct((512, 128), F32),
        in_specs=[smem] * 4 + [vmem] * 4 + [pl.BlockSpec(memory_space=pl.ANY)],
        out_specs=vmem,
        scratch_shapes=[
            pltpu.VMEM((512, 128), F32),
            pltpu.VMEM((512, 128), F32),
            pltpu.VMEM((8, 64, 128), F32),
            pltpu.VMEM((8, 64, 128), F32),
            pltpu.VMEM((128, 1024), BF16),
            pltpu.VMEM((8, 256, 128), F32),
            pltpu.VMEM((2, 4) + quarter, BF16),
            pltpu.VMEM((2, 2) + quarter, BF16),
            pltpu.VMEM((2,) + quarter, BF16),
            pltpu.VMEM((2,) + quarter, F32),
            pltpu.VMEM((2,) + quarter, BF16),
            pltpu.VMEM((2,) + quarter, BF16),
            pltpu.VMEM(quarter, BF16),
            pltpu.VMEM(quarter, BF16),
            pltpu.VMEM(quarter, BF16),
            pltpu.VMEM(quarter, BF16),
            pltpu.VMEM((32, 32, 128), F32),
            pltpu.VMEM((32, 2, 16, 128), F32),
            pltpu.VMEM((2,) + quarter, F32),
            pltpu.VMEM((2,) + quarter, BF16),
            pltpu.VMEM(quarter, BF16),
            pltpu.VMEM(quarter, BF16),
            pltpu.VMEM(quarter, BF16),
            pltpu.VMEM(quarter, BF16),
            pltpu.VMEM(quarter, BF16),
            pltpu.VMEM(quarter, BF16),
            pltpu.VMEM((8, 256, 128), BF16),
            pltpu.VMEM((512, 256), BF16),
            pltpu.SemaphoreType.DMA,
            pltpu.SemaphoreType.DMA((14,)),
            pltpu.SemaphoreType.DMA((14,)),
        ],
        compiler_params=pltpu.CompilerParams(collective_id=0, has_side_effects=True),
        name="mlfma",
    )(parent_of, octant_of, sources, kinds, rows, interp_theta.T, interp_phi.T, angle, planes)
    result = result.reshape(8, 2, 16, 2, 128).transpose(0, 1, 3, 2, 4)
    return result.reshape(1, 8, 2, 2, 2048)


def solution(mesh):
    placed = (
        P("wide", "narrow", None, None, None),
        P(),
        P(),
        P(),
        P(),
        P("wide", "narrow"),
        P("wide", "narrow"),
        P("wide", None, None),
        P("wide", None, None),
    )
    return jax.shard_map(
        body,
        mesh=mesh,
        in_specs=placed,
        out_specs=P("wide", "narrow", None, None, None),
        check_vma=False,
    )
```

```python
import functools

import jax
import jax.numpy as jnp
from jax import lax
from jax.experimental import pallas as pl
from jax.experimental.pallas import tpu as pltpu
from jax.sharding import PartitionSpec as P

MESH = pl.DeviceIdType.MESH
F32 = jnp.float32
BF16 = jnp.bfloat16


def iota(shape, dim):
    return lax.broadcasted_iota(jnp.int32, shape, dim)


def one_hot(mask):
    return jnp.where(mask, 1.0, 0.0).astype(BF16)


def dot(a, b, dims=((1,), (0,))):
    return lax.dot_general(a, b, (dims, ((), ())), preferred_element_type=F32)


def polar_matrices(theta_t):
    row = iota((64, 32), 0)
    pick_row = one_hot(iota((64, 32), 1) == 2 * (row & 15) + (row >> 5))
    full = dot(pick_row, theta_t)
    full = jnp.concatenate([full, full], axis=1)
    same = (iota((64, 128), 1) >> 6) == ((iota((64, 128), 0) >> 4) & 1)
    down = jnp.where(same, full, 0.0).astype(BF16)
    col = iota((32, 128), 1)
    pick_col = one_hot(iota((32, 128), 0) == 2 * ((col >> 1) & 15) + (col >> 6))
    spread = one_hot((iota((256, 64), 0) & 63) == iota((256, 64), 1))
    short = dot(theta_t, pick_col, ((0,), (0,))).astype(BF16)
    full = dot(spread, short)
    row, col = iota((256, 128), 0), iota((256, 128), 1)
    same = ((row >> 7) == ((col >> 5) & 1)) & (((row >> 6) & 1) == (col & 1))
    up = jnp.where(same, full, 0.0).astype(BF16)
    return up, down


def azimuth_up(phi_t):
    full = phi_t.astype(F32)
    full = jnp.concatenate([full, full], axis=1)
    full = jnp.concatenate([full, full], axis=0)
    same = (iota((128, 256), 0) >> 6) == (iota((128, 256), 1) >> 7)
    return jnp.where(same, full, 0.0).astype(BF16)


def azimuth_down(phi_t):
    spread = one_hot((iota((64, 128), 1) & 63) == iota((64, 128), 0))
    full = dot(phi_t, spread, ((0,), (0,)))
    full = jnp.concatenate([full, full], axis=0)
    same = (iota((256, 128), 0) >> 7) == (iota((256, 128), 1) >> 6)
    return jnp.where(same, full, 0.0).astype(BF16)


def cos_sin(angle):
    half = 0.5 * angle
    z = half * half
    sine, cosine = 1.0 / 6227020800.0, 1.0 / 479001600.0
    for below_sine, below_cosine in (
        (-1.0 / 39916800.0, -1.0 / 3628800.0),
        (1.0 / 362880.0, 1.0 / 40320.0),
        (-1.0 / 5040.0, -1.0 / 720.0),
        (1.0 / 120.0, 1.0 / 24.0),
        (-1.0 / 6.0, -0.5),
        (1.0, 1.0),
    ):
        sine = sine * z + below_sine
        cosine = cosine * z + below_cosine
    sine = sine * half
    twice = sine + sine
    return 1.0 - twice * sine, twice * cosine


def kernel(
    layers,
    parent_ref,
    octant_ref,
    source_ref,
    kind_ref,
    spec_ref,
    theta_ref,
    phi_ref,
    angle_ref,
    trans_hbm,
    out_ref,
    cos_rows,
    sin_rows,
    cos_tab,
    sin_tab,
    stacked,
    fine,
    part,
    gathered,
    own,
    below_0,
    below_1,
    above_0,
    above_1,
    trans_raw,
    trans,
    inc_own,
    inc_chip_0,
    inc_chip_1,
    inc_pair_0,
    inc_pair_1,
    inc_far_0,
    inc_far_1,
    back,
    sides,
    load_sem,
    send_sem,
    recv_sem,
):
    below, above = (below_0, below_1), (above_0, above_1)
    inc_chip, inc_pair, inc_far = (inc_chip_0, inc_chip_1), (inc_pair_0, inc_pair_1), (inc_far_0, inc_far_1)
    wide = lax.axis_index("wide")
    narrow = lax.axis_index("narrow")
    chip = narrow // 2
    core = narrow % 2
    odd = wide % 2
    turn = (wide // 2) % 2
    mine = (chip + turn) % 2
    theirs = 1 - mine
    pair_id = {"wide": wide, "narrow": 2 * chip + (1 - core)}
    chip_id = {"wide": wide, "narrow": 2 * (1 - chip) + core}
    far_id = {"wide": wide, "narrow": 2 * (1 - chip) + (1 - core)}
    up_id = {"wide": lax.rem(wide + 1, layers), "narrow": 2 * ((chip + odd) % 2) + core}
    down_id = {
        "wide": lax.rem(wide + layers - 1, layers),
        "narrow": 2 * ((chip + 1 - odd) % 2) + core,
    }
    has_up = wide < layers - 1
    has_down = wide > 0

    def greet(target):
        pl.semaphore_signal(barrier, inc=1, device_id=target, device_id_type=MESH)

    barrier = pltpu.get_barrier_semaphore()
    greet(pair_id)
    greet(chip_id)
    greet(far_id)

    @pl.when(has_up)
    def _():
        greet(up_id)

    @pl.when(has_down)
    def _():
        greet(down_id)

    quarter = 2 * core + mine
    load = pltpu.make_async_copy(
        trans_hbm.at[:, pl.ds(pl.multiple_of(quarter * 32, 32), 32), :], trans_raw, load_sem
    )
    load.start()

    def remote(slot, src, dst, target):
        return pltpu.make_async_remote_copy(
            src_ref=src,
            dst_ref=dst,
            send_sem=send_sem.at[slot],
            recv_sem=recv_sem.at[slot],
            device_id=target,
            device_id_type=MESH,
        )

    away = 2 * (1 - core)
    pair_quarter = away + mine
    chip_quarter = 2 * core + theirs
    far_quarter = away + theirs
    reduce_to = [
        [
            remote(3 * i + j, part.at[i, which], gathered.at[i, j], target)
            for j, (which, target) in enumerate(
                ((far_quarter, far_id), (chip_quarter, chip_id), (pair_quarter, pair_id))
            )
        ]
        for i in range(2)
    ]
    to_up = [remote(6 + i, own.at[i], below[i], up_id) for i in range(2)]
    to_down = [remote(8 + i, own.at[i], above[i], down_id) for i in range(2)]
    inc_to_chip = [remote(10 + i, inc_own.at[i], inc_chip[i], chip_id) for i in range(2)]
    inc_to_pair = [remote(12 + i, inc_own.at[i], inc_pair[i], pair_id) for i in range(2)]
    inc_forward = [remote(14 + i, inc_chip[i], inc_far[i], pair_id) for i in range(2)]

    polar_up, polar_down = polar_matrices(theta_ref[...])
    phi_t = phi_ref[...]
    coarse = dot(spec_ref[...], azimuth_up(phi_t)).astype(BF16)
    for child in range(8):
        for e in range(2):
            stacked[e * 64 : e * 64 + 64, child * 128 : child * 128 + 128] = coarse[
                child * 64 : child * 64 + 64, e * 128 : e * 128 + 128
            ]
    raised = dot(polar_up, stacked[...])
    for child in range(8):
        fine[child] = raised[:, child * 128 : child * 128 + 128]

    cos_rows[...], sin_rows[...] = cos_sin(angle_ref[...])
    for rows_of, tab in ((cos_rows, cos_tab), (sin_rows, sin_tab)):
        for octant in range(8):
            tab[octant] = rows_of[pl.ds(octant, 64, stride=8), :]

    def partials(i, which):
        rows = pl.ds(pl.multiple_of(which * 16, 16), 16)

        def add(step, sums):
            sums = list(sums)
            for child in (4 * step, 4 * step + 1, 4 * step + 2, 4 * step + 3):
                octant = octant_ref[0, child]
                home = parent_ref[0, child]
                real = fine[child, pl.ds(pl.multiple_of(i * 64 + which * 16, 16), 16), :]
                imag = fine[child, pl.ds(pl.multiple_of(128 + i * 64 + which * 16, 16), 16), :]
                cosine = cos_tab[octant, rows, :]
                sine = sin_tab[octant, rows, :]
                turned_real = real * cosine - imag * sine
                turned_imag = real * sine + imag * cosine
                for parent in range(4):
                    weight = jnp.where(home == parent, 1.0, 0.0)
                    sums[2 * parent] = sums[2 * parent] + weight * turned_real
                    sums[2 * parent + 1] = sums[2 * parent + 1] + weight * turned_imag
            return tuple(sums)

        sums = lax.fori_loop(0, 2, add, tuple(jnp.zeros((16, 128), F32) for _ in range(8)))
        for parent in range(4):
            part[i, which, parent, 0] = sums[2 * parent].astype(BF16)
            part[i, which, parent, 1] = sums[2 * parent + 1].astype(BF16)

    for i in range(2):
        for j, which in enumerate((far_quarter, chip_quarter, pair_quarter)):
            partials(i, which)
            if i == 0 and j == 0:
                greeted = 3 + has_up.astype(jnp.int32) + has_down.astype(jnp.int32)
                pl.semaphore_wait(barrier, greeted)
            reduce_to[i][j].start()
    for i in range(2):
        partials(i, quarter)

    load.wait()

    def split(kind, carry):
        for t in range(2):
            trans[kind, t] = trans_raw[kind, pl.ds(t, 16, stride=2), :]
        return carry

    lax.fori_loop(0, 32, split, 0)
    down = azimuth_down(phi_t)

    @pl.when(wide == 0)
    def _():
        for ref in below:
            ref[...] = jnp.zeros_like(ref)

    @pl.when(wide == layers - 1)
    def _():
        for ref in above:
            ref[...] = jnp.zeros_like(ref)

    for i in range(2):
        total = part[i, quarter].astype(F32)
        for j in (2, 1, 0):
            reduce_to[i][j].wait_recv()
            total = total + gathered[i, j].astype(F32)
        own[i] = total.astype(BF16)

        @pl.when(has_up)
        def _():
            to_up[i].start()

        @pl.when(has_down)
        def _():
            to_down[i].start()

    for i in range(2):

        @pl.when(has_down)
        def _():
            to_up[i].wait_recv()

        @pl.when(has_up)
        def _():
            to_down[i].wait_recv()

        pools = (below[i], below[i], own.at[i], own.at[i], above[i], above[i])
        for parent in range(4):
            real_sum = jnp.zeros((16, 128), F32)
            imag_sum = jnp.zeros((16, 128), F32)
            for column, pool in enumerate(pools):
                source = lax.rem(source_ref[0, parent, column], 4)
                kind = kind_ref[0, parent, column]
                table_real = trans[kind, 0]
                table_imag = trans[kind, 1]
                real = pool[source, 0].astype(F32)
                imag = pool[source, 1].astype(F32)
                real_sum = real_sum + table_real * real - table_imag * imag
                imag_sum = imag_sum + table_real * imag + table_imag * real
            inc_own[i, parent, 0] = real_sum.astype(BF16)
            inc_own[i, parent, 1] = imag_sum.astype(BF16)
        inc_to_chip[i].start()
        inc_to_pair[i].start()

    def turn_back(i, values, which):
        rows = pl.ds(pl.multiple_of(which * 16, 16), 16)

        def one(step, carry):
            for child in (4 * step, 4 * step + 1, 4 * step + 2, 4 * step + 3):
                home = parent_ref[0, child]
                octant = octant_ref[0, child]
                cosine = cos_tab[octant, rows, :]
                sine = sin_tab[octant, rows, :]
                real = values[home, 0].astype(F32)
                imag = values[home, 1].astype(F32)
                lanes = pl.ds(pl.multiple_of(child * 128, 128), 128)
                back[i, pl.ds(pl.multiple_of(which * 16, 16), 16), lanes] = (
                    real * cosine + imag * sine
                ).astype(BF16)
                back[i, pl.ds(pl.multiple_of(64 + which * 16, 16), 16), lanes] = (
                    imag * cosine - real * sine
                ).astype(BF16)
            return carry

        lax.fori_loop(0, 2, one, 0)

    for i in range(2):
        turn_back(i, inc_own.at[i], quarter)
    for i in range(2):
        inc_to_pair[i].wait_recv()
        turn_back(i, inc_pair[i], pair_quarter)
    for i in range(2):
        inc_to_chip[i].wait_recv()
        inc_forward[i].start()
        turn_back(i, inc_chip[i], chip_quarter)

    for i in range(2):
        inc_forward[i].wait_recv()
        turn_back(i, inc_far[i], far_quarter)
        lowered = dot(polar_down, back[i]).astype(BF16)
        for child in range(8):
            for e in range(2):
                sides[i, child * 32 : child * 32 + 32, e * 128 : e * 128 + 128] = lowered[
                    e * 32 : e * 32 + 32, child * 128 : child * 128 + 128
                ]
        out_ref[pl.ds(i, 256, stride=2), :] = dot(sides[i], down)

    for i in range(2):
        for copy in (*reduce_to[i], inc_to_chip[i], inc_to_pair[i], inc_forward[i]):
            copy.wait_send()

        @pl.when(has_up)
        def _():
            to_up[i].wait_send()

        @pl.when(has_down)
        def _():
            to_down[i].wait_send()


def body(
    child_spec,
    interp_theta,
    interp_phi,
    shift_angle,
    trans_op,
    parent_of,
    octant_of,
    sources,
    kinds,
):
    layers = lax.axis_size("wide")
    rows = child_spec.reshape(8, 2, 2, 16, 128).transpose(0, 1, 3, 2, 4).reshape(512, 128)
    angle = shift_angle.reshape(8, 64, 128).transpose(1, 0, 2).reshape(512, 128)
    planes = trans_op.reshape(32, 2, 64, 128).transpose(0, 2, 1, 3).reshape(32, 128, 128)
    quarter = (4, 2, 16, 128)
    vmem = pl.BlockSpec(memory_space=pltpu.VMEM)
    smem = pl.BlockSpec(memory_space=pltpu.SMEM)
    result = pl.pallas_call(
        functools.partial(kernel, layers),
        out_shape=pltpu.VMEM((512, 128), F32),
        in_specs=[smem] * 4 + [vmem] * 4 + [pl.BlockSpec(memory_space=pl.ANY)],
        out_specs=vmem,
        scratch_shapes=[
            pltpu.VMEM((512, 128), F32),
            pltpu.VMEM((512, 128), F32),
            pltpu.VMEM((8, 64, 128), F32),
            pltpu.VMEM((8, 64, 128), F32),
            pltpu.VMEM((128, 1024), BF16),
            pltpu.VMEM((8, 256, 128), F32),
            pltpu.VMEM((2, 4) + quarter, BF16),
            pltpu.VMEM((2, 3) + quarter, BF16),
            pltpu.VMEM((2,) + quarter, BF16),
            pltpu.VMEM(quarter, BF16),
            pltpu.VMEM(quarter, BF16),
            pltpu.VMEM(quarter, BF16),
            pltpu.VMEM(quarter, BF16),
            pltpu.VMEM((32, 32, 128), F32),
            pltpu.VMEM((32, 2, 16, 128), F32),
            pltpu.VMEM((2,) + quarter, BF16),
            pltpu.VMEM(quarter, BF16),
            pltpu.VMEM(quarter, BF16),
            pltpu.VMEM(quarter, BF16),
            pltpu.VMEM(quarter, BF16),
            pltpu.VMEM(quarter, BF16),
            pltpu.VMEM(quarter, BF16),
            pltpu.VMEM((2, 128, 1024), BF16),
            pltpu.VMEM((2, 256, 256), BF16),
            pltpu.SemaphoreType.DMA,
            pltpu.SemaphoreType.DMA((16,)),
            pltpu.SemaphoreType.DMA((16,)),
        ],
        compiler_params=pltpu.CompilerParams(collective_id=0, has_side_effects=True),
        name="mlfma",
    )(parent_of, octant_of, sources, kinds, rows, interp_theta.T, interp_phi.T, angle, planes)
    result = result.reshape(8, 2, 16, 2, 128).transpose(0, 1, 3, 2, 4)
    return result.reshape(1, 8, 2, 2, 2048)


def solution(mesh):
    placed = (
        P("wide", "narrow", None, None, None),
        P(),
        P(),
        P(),
        P(),
        P("wide", "narrow"),
        P("wide", "narrow"),
        P("wide", None, None),
        P("wide", None, None),
    )
    return jax.shard_map(
        body,
        mesh=mesh,
        in_specs=placed,
        out_specs=P("wide", "narrow", None, None, None),
        check_vma=False,
    )
```

```python
import functools

import jax
import jax.numpy as jnp
from jax import lax
from jax.experimental import pallas as pl
from jax.experimental.pallas import tpu as pltpu
from jax.sharding import PartitionSpec as P

MESH = pl.DeviceIdType.MESH
F32 = jnp.float32
BF16 = jnp.bfloat16


def iota(shape, dim):
    return lax.broadcasted_iota(jnp.int32, shape, dim)


def one_hot(mask):
    return jnp.where(mask, 1.0, 0.0).astype(BF16)


def dot(a, b, dims=((1,), (0,))):
    return lax.dot_general(a, b, (dims, ((), ())), preferred_element_type=F32)


def polar_matrices(theta_t):
    row = iota((64, 32), 0)
    pick_row = one_hot(iota((64, 32), 1) == 2 * (row & 15) + (row >> 5))
    full = dot(pick_row, theta_t)
    full = jnp.concatenate([full, full], axis=1)
    same = (iota((64, 128), 1) >> 6) == ((iota((64, 128), 0) >> 4) & 1)
    down = jnp.where(same, full, 0.0).astype(BF16)
    col = iota((32, 128), 1)
    pick_col = one_hot(iota((32, 128), 0) == 2 * ((col >> 1) & 15) + (col >> 6))
    spread = one_hot((iota((256, 64), 0) & 63) == iota((256, 64), 1))
    short = dot(theta_t, pick_col, ((0,), (0,))).astype(BF16)
    full = dot(spread, short)
    row, col = iota((256, 128), 0), iota((256, 128), 1)
    same = ((row >> 7) == ((col >> 5) & 1)) & (((row >> 6) & 1) == (col & 1))
    up = jnp.where(same, full, 0.0).astype(BF16)
    return up, down


def azimuth_up(phi_t):
    full = phi_t.astype(F32)
    full = jnp.concatenate([full, full], axis=1)
    full = jnp.concatenate([full, full], axis=0)
    same = (iota((128, 256), 0) >> 6) == (iota((128, 256), 1) >> 7)
    return jnp.where(same, full, 0.0).astype(BF16)


def azimuth_down(phi_t):
    spread = one_hot((iota((64, 128), 1) & 63) == iota((64, 128), 0))
    full = dot(phi_t, spread, ((0,), (0,)))
    full = jnp.concatenate([full, full], axis=0)
    same = (iota((256, 128), 0) >> 7) == (iota((256, 128), 1) >> 6)
    return jnp.where(same, full, 0.0).astype(BF16)


def cos_sin(angle):
    half = 0.5 * angle
    z = half * half
    sine, cosine = 1.0 / 6227020800.0, 1.0 / 479001600.0
    for below_sine, below_cosine in (
        (-1.0 / 39916800.0, -1.0 / 3628800.0),
        (1.0 / 362880.0, 1.0 / 40320.0),
        (-1.0 / 5040.0, -1.0 / 720.0),
        (1.0 / 120.0, 1.0 / 24.0),
        (-1.0 / 6.0, -0.5),
        (1.0, 1.0),
    ):
        sine = sine * z + below_sine
        cosine = cosine * z + below_cosine
    sine = sine * half
    twice = sine + sine
    return 1.0 - twice * sine, twice * cosine


def kernel(
    layers,
    parent_ref,
    octant_ref,
    source_ref,
    kind_ref,
    spec_ref,
    theta_ref,
    phi_ref,
    angle_ref,
    trans_hbm,
    out_ref,
    cos_rows,
    sin_rows,
    cos_tab,
    sin_tab,
    stacked,
    fine,
    part,
    pair_in,
    chip_out,
    chip_in,
    own,
    trans_raw,
    trans,
    inc_own,
    back,
    sides,
    load_sem,
    send_sem,
    recv_sem,
    *arrivals,
):
    below, above, inc_pair = arrivals[0:4], arrivals[4:8], arrivals[8:12]
    wide = lax.axis_index("wide")
    narrow = lax.axis_index("narrow")
    chip = narrow // 2
    core = narrow % 2
    odd = wide % 2
    pair_id = {"wide": wide, "narrow": 2 * chip + (1 - core)}
    chip_id = {"wide": wide, "narrow": 2 * (1 - chip) + core}
    up_id = {"wide": lax.rem(wide + 1, layers), "narrow": 2 * ((chip + odd) % 2) + core}
    down_id = {
        "wide": lax.rem(wide + layers - 1, layers),
        "narrow": 2 * ((chip + 1 - odd) % 2) + core,
    }
    has_up = wide < layers - 1
    has_down = wide > 0

    def greet(target):
        pl.semaphore_signal(barrier, inc=1, device_id=target, device_id_type=MESH)

    barrier = pltpu.get_barrier_semaphore()
    greet(pair_id)
    greet(chip_id)

    @pl.when(has_up)
    def _():
        greet(up_id)

    @pl.when(has_down)
    def _():
        greet(down_id)

    load = pltpu.make_async_copy(
        trans_hbm.at[:, pl.ds(pl.multiple_of(core * 64, 64), 64), :], trans_raw, load_sem
    )
    load.start()

    def remote(slot, src, dst, target):
        return pltpu.make_async_remote_copy(
            src_ref=src,
            dst_ref=dst,
            send_sem=send_sem.at[slot],
            recv_sem=recv_sem.at[slot],
            device_id=target,
            device_id_type=MESH,
        )

    home_quarter = 2 * core
    away_quarter = 2 * (1 - core)
    chunks = [(i, g) for i in range(2) for g in range(2)]
    to_pair, to_chip, to_up, to_down, inc_to_pair = [], [], [], [], []
    for c, (i, g) in enumerate(chunks):
        to_pair.append(remote(c, part.at[i, away_quarter + g], pair_in.at[c], pair_id))
        to_chip.append(remote(4 + c, chip_out.at[c], chip_in.at[c], chip_id))
        to_up.append(remote(8 + c, own.at[c], below[c], up_id))
        to_down.append(remote(12 + c, own.at[c], above[c], down_id))
        inc_to_pair.append(remote(16 + c, inc_own.at[c], inc_pair[c], pair_id))

    polar_up, polar_down = polar_matrices(theta_ref[...])
    phi_t = phi_ref[...]
    coarse = dot(spec_ref[...], azimuth_up(phi_t)).astype(BF16)
    for child in range(8):
        for e in range(2):
            stacked[e * 64 : e * 64 + 64, child * 128 : child * 128 + 128] = coarse[
                child * 64 : child * 64 + 64, e * 128 : e * 128 + 128
            ]
    raised = dot(polar_up, stacked[...])
    for child in range(8):
        fine[child] = raised[:, child * 128 : child * 128 + 128]

    cos_rows[...], sin_rows[...] = cos_sin(angle_ref[...])
    for rows_of, tab in ((cos_rows, cos_tab), (sin_rows, sin_tab)):
        for octant in range(8):
            tab[octant] = rows_of[pl.ds(octant, 64, stride=8), :]

    def partials(i, which):
        rows = pl.ds(pl.multiple_of(which * 16, 16), 16)

        def add(step, sums):
            sums = list(sums)
            for child in (4 * step, 4 * step + 1, 4 * step + 2, 4 * step + 3):
                octant = octant_ref[0, child]
                home = parent_ref[0, child]
                real = fine[child, pl.ds(pl.multiple_of(i * 64 + which * 16, 16), 16), :]
                imag = fine[child, pl.ds(pl.multiple_of(128 + i * 64 + which * 16, 16), 16), :]
                cosine = cos_tab[octant, rows, :]
                sine = sin_tab[octant, rows, :]
                turned_real = real * cosine - imag * sine
                turned_imag = real * sine + imag * cosine
                for parent in range(4):
                    weight = jnp.where(home == parent, 1.0, 0.0)
                    sums[2 * parent] = sums[2 * parent] + weight * turned_real
                    sums[2 * parent + 1] = sums[2 * parent + 1] + weight * turned_imag
            return tuple(sums)

        sums = lax.fori_loop(0, 2, add, tuple(jnp.zeros((16, 128), F32) for _ in range(8)))
        for parent in range(4):
            part[i, which, parent, 0] = sums[2 * parent].astype(BF16)
            part[i, which, parent, 1] = sums[2 * parent + 1].astype(BF16)

    for c, (i, g) in enumerate(chunks):
        partials(i, away_quarter + g)
        if c == 0:
            greeted = 2 + has_up.astype(jnp.int32) + has_down.astype(jnp.int32)
            pl.semaphore_wait(barrier, greeted)
        to_pair[c].start()
    for c, (i, g) in enumerate(chunks):
        partials(i, home_quarter + g)
        to_pair[c].wait_recv()
        chip_out[c] = (part[i, home_quarter + g].astype(F32) + pair_in[c].astype(F32)).astype(BF16)
        to_chip[c].start()

    load.wait()

    def split(kind, carry):
        for t in range(2):
            trans[kind, t] = trans_raw[kind, pl.ds(t, 32, stride=2), :]
        return carry

    lax.fori_loop(0, 32, split, 0)
    down = azimuth_down(phi_t)

    @pl.when(wide == 0)
    def _():
        for ref in below:
            ref[...] = jnp.zeros_like(ref)

    @pl.when(wide == layers - 1)
    def _():
        for ref in above:
            ref[...] = jnp.zeros_like(ref)

    for c in range(4):
        to_chip[c].wait_recv()
        own[c] = (chip_out[c].astype(F32) + chip_in[c].astype(F32)).astype(BF16)

        @pl.when(has_up)
        def _():
            to_up[c].start()

        @pl.when(has_down)
        def _():
            to_down[c].start()

    for c, (i, g) in enumerate(chunks):

        @pl.when(has_down)
        def _():
            to_up[c].wait_recv()

        @pl.when(has_up)
        def _():
            to_down[c].wait_recv()

        pools = (below[c], below[c], own.at[c], own.at[c], above[c], above[c])
        for parent in range(4):
            real_sum = jnp.zeros((16, 128), F32)
            imag_sum = jnp.zeros((16, 128), F32)
            for column, pool in enumerate(pools):
                source = lax.rem(source_ref[0, parent, column], 4)
                kind = kind_ref[0, parent, column]
                table_real = trans[kind, 0, g * 16 : g * 16 + 16, :]
                table_imag = trans[kind, 1, g * 16 : g * 16 + 16, :]
                real = pool[source, 0].astype(F32)
                imag = pool[source, 1].astype(F32)
                real_sum = real_sum + table_real * real - table_imag * imag
                imag_sum = imag_sum + table_real * imag + table_imag * real
            inc_own[c, parent, 0] = real_sum.astype(BF16)
            inc_own[c, parent, 1] = imag_sum.astype(BF16)
        inc_to_pair[c].start()

    def turn_back(i, values, which):
        rows = pl.ds(pl.multiple_of(which * 16, 16), 16)

        def one(step, carry):
            for child in (4 * step, 4 * step + 1, 4 * step + 2, 4 * step + 3):
                home = parent_ref[0, child]
                octant = octant_ref[0, child]
                cosine = cos_tab[octant, rows, :]
                sine = sin_tab[octant, rows, :]
                real = values[home, 0].astype(F32)
                imag = values[home, 1].astype(F32)
                lanes = pl.ds(pl.multiple_of(child * 128, 128), 128)
                back[i, pl.ds(pl.multiple_of(which * 16, 16), 16), lanes] = (
                    real * cosine + imag * sine
                ).astype(BF16)
                back[i, pl.ds(pl.multiple_of(64 + which * 16, 16), 16), lanes] = (
                    imag * cosine - real * sine
                ).astype(BF16)
            return carry

        lax.fori_loop(0, 2, one, 0)

    for c, (i, g) in enumerate(chunks):
        turn_back(i, inc_own.at[c], home_quarter + g)

    for i in range(2):
        for g in range(2):
            inc_to_pair[2 * i + g].wait_recv()
            turn_back(i, inc_pair[2 * i + g], away_quarter + g)
        lowered = dot(polar_down, back[i]).astype(BF16)
        for child in range(8):
            for e in range(2):
                sides[i, child * 32 : child * 32 + 32, e * 128 : e * 128 + 128] = lowered[
                    e * 32 : e * 32 + 32, child * 128 : child * 128 + 128
                ]
        out_ref[pl.ds(i, 256, stride=2), :] = dot(sides[i], down)

    for c in range(4):
        for copy in (to_pair[c], to_chip[c], inc_to_pair[c]):
            copy.wait_send()

        @pl.when(has_up)
        def _():
            to_up[c].wait_send()

        @pl.when(has_down)
        def _():
            to_down[c].wait_send()


def body(
    child_spec,
    interp_theta,
    interp_phi,
    shift_angle,
    trans_op,
    parent_of,
    octant_of,
    sources,
    kinds,
):
    layers = lax.axis_size("wide")
    rows = child_spec.reshape(8, 2, 2, 16, 128).transpose(0, 1, 3, 2, 4).reshape(512, 128)
    angle = shift_angle.reshape(8, 64, 128).transpose(1, 0, 2).reshape(512, 128)
    planes = trans_op.reshape(32, 2, 64, 128).transpose(0, 2, 1, 3).reshape(32, 128, 128)
    quarter = (4, 2, 16, 128)
    vmem = pl.BlockSpec(memory_space=pltpu.VMEM)
    smem = pl.BlockSpec(memory_space=pltpu.SMEM)
    result = pl.pallas_call(
        functools.partial(kernel, layers),
        out_shape=pltpu.VMEM((512, 128), F32),
        in_specs=[smem] * 4 + [vmem] * 4 + [pl.BlockSpec(memory_space=pl.ANY)],
        out_specs=vmem,
        scratch_shapes=[
            pltpu.VMEM((512, 128), F32),
            pltpu.VMEM((512, 128), F32),
            pltpu.VMEM((8, 64, 128), F32),
            pltpu.VMEM((8, 64, 128), F32),
            pltpu.VMEM((128, 1024), BF16),
            pltpu.VMEM((8, 256, 128), F32),
            pltpu.VMEM((2, 4) + quarter, BF16),
            pltpu.VMEM((4,) + quarter, BF16),
            pltpu.VMEM((4,) + quarter, BF16),
            pltpu.VMEM((4,) + quarter, BF16),
            pltpu.VMEM((4,) + quarter, BF16),
            pltpu.VMEM((32, 64, 128), F32),
            pltpu.VMEM((32, 2, 32, 128), F32),
            pltpu.VMEM((4,) + quarter, BF16),
            pltpu.VMEM((2, 128, 1024), BF16),
            pltpu.VMEM((2, 256, 256), BF16),
            pltpu.SemaphoreType.DMA,
            pltpu.SemaphoreType.DMA((20,)),
            pltpu.SemaphoreType.DMA((20,)),
        ]
        + [pltpu.VMEM(quarter, BF16)] * 12,
        compiler_params=pltpu.CompilerParams(collective_id=0, has_side_effects=True),
        name="mlfma",
    )(parent_of, octant_of, sources, kinds, rows, interp_theta.T, interp_phi.T, angle, planes)
    result = result.reshape(8, 2, 16, 2, 128).transpose(0, 1, 3, 2, 4)
    return result.reshape(1, 8, 2, 2, 2048)


def solution(mesh):
    placed = (
        P("wide", "narrow", None, None, None),
        P(),
        P(),
        P(),
        P(),
        P("wide", "narrow"),
        P("wide", "narrow"),
        P("wide", None, None),
        P("wide", None, None),
    )
    return jax.shard_map(
        body,
        mesh=mesh,
        in_specs=placed,
        out_specs=P("wide", "narrow", None, None, None),
        check_vma=False,
    )
```

```python
import functools

import jax
import jax.numpy as jnp
from jax import lax
from jax.experimental import pallas as pl
from jax.experimental.pallas import tpu as pltpu
from jax.sharding import PartitionSpec as P

MESH = pl.DeviceIdType.MESH
F32 = jnp.float32
BF16 = jnp.bfloat16


def iota(shape, dim):
    return lax.broadcasted_iota(jnp.int32, shape, dim)


def one_hot(mask):
    return jnp.where(mask, 1.0, 0.0).astype(BF16)


def dot(a, b, dims=((1,), (0,))):
    return lax.dot_general(a, b, (dims, ((), ())), preferred_element_type=F32)


def polar_matrices(theta_t):
    row = iota((64, 32), 0)
    pick_row = one_hot(iota((64, 32), 1) == 2 * (row & 15) + (row >> 5))
    full = dot(pick_row, theta_t)
    full = jnp.concatenate([full, full], axis=1)
    same = (iota((64, 128), 1) >> 6) == ((iota((64, 128), 0) >> 4) & 1)
    down = jnp.where(same, full, 0.0).astype(BF16)
    col = iota((32, 128), 1)
    pick_col = one_hot(iota((32, 128), 0) == 2 * ((col >> 1) & 15) + (col >> 6))
    short = dot(theta_t, pick_col, ((0,), (0,)))
    full = jnp.concatenate([short] * 4, axis=0)
    row, col = iota((256, 128), 0), iota((256, 128), 1)
    same = ((row >> 7) == ((col >> 5) & 1)) & (((row >> 6) & 1) == (col & 1))
    up = jnp.where(same, full, 0.0).astype(BF16)
    return up, down


def azimuth_up(phi_t):
    full = phi_t.astype(F32)
    full = jnp.concatenate([full, full], axis=1)
    full = jnp.concatenate([full, full], axis=0)
    same = (iota((128, 256), 0) >> 6) == (iota((128, 256), 1) >> 7)
    return jnp.where(same, full, 0.0).astype(BF16)


def azimuth_down(phi_t):
    spread = one_hot((iota((64, 128), 1) & 63) == iota((64, 128), 0))
    full = dot(phi_t, spread, ((0,), (0,)))
    full = jnp.concatenate([full, full], axis=0)
    same = (iota((256, 128), 0) >> 7) == (iota((256, 128), 1) >> 6)
    return jnp.where(same, full, 0.0).astype(BF16)


def cos_sin(angle):
    half = 0.5 * angle
    z = half * half
    sine, cosine = 1.0 / 6227020800.0, 1.0 / 479001600.0
    for below_sine, below_cosine in (
        (-1.0 / 39916800.0, -1.0 / 3628800.0),
        (1.0 / 362880.0, 1.0 / 40320.0),
        (-1.0 / 5040.0, -1.0 / 720.0),
        (1.0 / 120.0, 1.0 / 24.0),
        (-1.0 / 6.0, -0.5),
        (1.0, 1.0),
    ):
        sine = sine * z + below_sine
        cosine = cosine * z + below_cosine
    sine = sine * half
    twice = sine + sine
    return 1.0 - twice * sine, twice * cosine


def kernel(
    layers,
    parent_hbm,
    octant_hbm,
    source_hbm,
    kind_hbm,
    spec_hbm,
    theta_hbm,
    phi_hbm,
    angle_hbm,
    trans_hbm,
    out_ref,
    parent_ref,
    octant_ref,
    source_ref,
    kind_ref,
    spec_ref,
    theta_ref,
    phi_ref,
    angle_ref,
    input_sem,
    cos_tab,
    sin_tab,
    fine,
    part,
    pair_in,
    chip_out,
    chip_in,
    own,
    trans_raw,
    trans,
    inc_own,
    back,
    sides,
    load_sem,
    send_sem,
    recv_sem,
    *arrivals,
):
    inputs = [
        pltpu.make_async_copy(src, dst, input_sem.at[slot])
        for slot, (src, dst) in enumerate(
            (
                (theta_hbm, theta_ref),
                (phi_hbm, phi_ref),
                (spec_hbm, spec_ref),
                (angle_hbm, angle_ref),
                (parent_hbm, parent_ref),
                (octant_hbm, octant_ref),
                (source_hbm, source_ref),
                (kind_hbm, kind_ref),
            )
        )
    ]
    for copy in inputs:
        copy.start()
    below, above, inc_pair = arrivals[0:4], arrivals[4:8], arrivals[8:12]
    wide = lax.axis_index("wide")
    narrow = lax.axis_index("narrow")
    chip = narrow // 2
    core = narrow % 2
    odd = wide % 2
    pair_id = {"wide": wide, "narrow": 2 * chip + (1 - core)}
    chip_id = {"wide": wide, "narrow": 2 * (1 - chip) + core}
    up_id = {"wide": lax.rem(wide + 1, layers), "narrow": 2 * ((chip + odd) % 2) + core}
    down_id = {
        "wide": lax.rem(wide + layers - 1, layers),
        "narrow": 2 * ((chip + 1 - odd) % 2) + core,
    }
    has_up = wide < layers - 1
    has_down = wide > 0

    def greet(target):
        pl.semaphore_signal(barrier, inc=1, device_id=target, device_id_type=MESH)

    barrier = pltpu.get_barrier_semaphore()
    greet(pair_id)
    greet(chip_id)

    @pl.when(has_up)
    def _():
        greet(up_id)

    @pl.when(has_down)
    def _():
        greet(down_id)

    load = pltpu.make_async_copy(
        trans_hbm.at[:, pl.ds(pl.multiple_of(core * 64, 64), 64), :], trans_raw, load_sem
    )

    load.start()

    def remote(slot, src, dst, target):
        return pltpu.make_async_remote_copy(
            src_ref=src,
            dst_ref=dst,
            send_sem=send_sem.at[slot],
            recv_sem=recv_sem.at[slot],
            device_id=target,
            device_id_type=MESH,
        )

    home_quarter = 2 * core
    away_quarter = 2 * (1 - core)
    chunks = [(i, g) for i in range(2) for g in range(2)]
    to_pair, to_chip, to_up, to_down, inc_to_pair = [], [], [], [], []
    for c, (i, g) in enumerate(chunks):
        to_pair.append(remote(c, part.at[i, away_quarter + g], pair_in.at[c], pair_id))
        to_chip.append(remote(4 + c, chip_out.at[c], chip_in.at[c], chip_id))
        to_up.append(remote(8 + c, own.at[c], below[c], up_id))
        to_down.append(remote(12 + c, own.at[c], above[c], down_id))
        inc_to_pair.append(remote(16 + c, inc_own.at[c], inc_pair[c], pair_id))

    inputs[0].wait()
    polar_up, polar_down = polar_matrices(theta_ref[...])
    for copy in inputs[1:]:
        copy.wait()
    phi_t = phi_ref[...]
    azimuth = azimuth_up(phi_t)
    for child in range(8):
        coarse = dot(spec_ref[child * 64 : child * 64 + 64, :], azimuth).astype(BF16)
        coarse = jnp.concatenate([coarse[:, 0:128], coarse[:, 128:256]], axis=0)
        fine[child] = dot(polar_up, coarse)
        angle = angle_ref[pl.ds(child, 64, stride=8), :]
        cos_tab[child], sin_tab[child] = cos_sin(angle)

    def partials(i, which):
        rows = pl.ds(pl.multiple_of(which * 16, 16), 16)

        def add(step, sums):
            sums = list(sums)
            for child in (4 * step, 4 * step + 1, 4 * step + 2, 4 * step + 3):
                octant = octant_ref[0, child]
                home = parent_ref[0, child]
                real = fine[child, pl.ds(pl.multiple_of(i * 64 + which * 16, 16), 16), :]
                imag = fine[child, pl.ds(pl.multiple_of(128 + i * 64 + which * 16, 16), 16), :]
                cosine = cos_tab[octant, rows, :]
                sine = sin_tab[octant, rows, :]
                turned_real = real * cosine - imag * sine
                turned_imag = real * sine + imag * cosine
                for parent in range(4):
                    weight = jnp.where(home == parent, 1.0, 0.0)
                    sums[2 * parent] = sums[2 * parent] + weight * turned_real
                    sums[2 * parent + 1] = sums[2 * parent + 1] + weight * turned_imag
            return tuple(sums)

        sums = lax.fori_loop(0, 2, add, tuple(jnp.zeros((16, 128), F32) for _ in range(8)))
        for parent in range(4):
            part[i, which, parent, 0] = sums[2 * parent].astype(BF16)
            part[i, which, parent, 1] = sums[2 * parent + 1].astype(BF16)

    for c, (i, g) in enumerate(chunks):
        partials(i, away_quarter + g)
        if c == 0:
            greeted = 2 + has_up.astype(jnp.int32) + has_down.astype(jnp.int32)
            pl.semaphore_wait(barrier, greeted)
        to_pair[c].start()
    for c, (i, g) in enumerate(chunks):
        partials(i, home_quarter + g)
        to_pair[c].wait_recv()
        chip_out[c] = (part[i, home_quarter + g].astype(F32) + pair_in[c].astype(F32)).astype(BF16)
        to_chip[c].start()

    load.wait()

    def split(kind, carry):
        for t in range(2):
            trans[kind, t] = trans_raw[kind, pl.ds(t, 32, stride=2), :]
        return carry

    lax.fori_loop(0, 32, split, 0)
    down = azimuth_down(phi_t)

    @pl.when(wide == 0)
    def _():
        for ref in below:
            ref[...] = jnp.zeros_like(ref)

    @pl.when(wide == layers - 1)
    def _():
        for ref in above:
            ref[...] = jnp.zeros_like(ref)

    for c in range(4):
        to_chip[c].wait_recv()
        own[c] = (chip_out[c].astype(F32) + chip_in[c].astype(F32)).astype(BF16)

        @pl.when(has_up)
        def _():
            to_up[c].start()

        @pl.when(has_down)
        def _():
            to_down[c].start()

    for c, (i, g) in enumerate(chunks):

        @pl.when(has_down)
        def _():
            to_up[c].wait_recv()

        @pl.when(has_up)
        def _():
            to_down[c].wait_recv()

        pools = (below[c], below[c], own.at[c], own.at[c], above[c], above[c])
        for parent in range(4):
            real_sum = jnp.zeros((16, 128), F32)
            imag_sum = jnp.zeros((16, 128), F32)
            for column, pool in enumerate(pools):
                source = lax.rem(source_ref[0, parent, column], 4)
                kind = kind_ref[0, parent, column]
                table_real = trans[kind, 0, g * 16 : g * 16 + 16, :]
                table_imag = trans[kind, 1, g * 16 : g * 16 + 16, :]
                real = pool[source, 0].astype(F32)
                imag = pool[source, 1].astype(F32)
                real_sum = real_sum + table_real * real - table_imag * imag
                imag_sum = imag_sum + table_real * imag + table_imag * real
            inc_own[c, parent, 0] = real_sum.astype(BF16)
            inc_own[c, parent, 1] = imag_sum.astype(BF16)
        inc_to_pair[c].start()

    def turn_back(i, values, which):
        rows = pl.ds(pl.multiple_of(which * 16, 16), 16)

        def one(step, carry):
            for child in (4 * step, 4 * step + 1, 4 * step + 2, 4 * step + 3):
                home = parent_ref[0, child]
                octant = octant_ref[0, child]
                cosine = cos_tab[octant, rows, :]
                sine = sin_tab[octant, rows, :]
                real = values[home, 0].astype(F32)
                imag = values[home, 1].astype(F32)
                lanes = pl.ds(pl.multiple_of(child * 128, 128), 128)
                back[i, pl.ds(pl.multiple_of(which * 16, 16), 16), lanes] = (
                    real * cosine + imag * sine
                ).astype(BF16)
                back[i, pl.ds(pl.multiple_of(64 + which * 16, 16), 16), lanes] = (
                    imag * cosine - real * sine
                ).astype(BF16)
            return carry

        lax.fori_loop(0, 2, one, 0)

    for c, (i, g) in enumerate(chunks):
        turn_back(i, inc_own.at[c], home_quarter + g)

    for i in range(2):
        for g in range(2):
            inc_to_pair[2 * i + g].wait_recv()
            turn_back(i, inc_pair[2 * i + g], away_quarter + g)
        lowered = dot(polar_down, back[i]).astype(BF16)
        for child in range(8):
            for e in range(2):
                sides[i, child * 32 : child * 32 + 32, e * 128 : e * 128 + 128] = lowered[
                    e * 32 : e * 32 + 32, child * 128 : child * 128 + 128
                ]
        out_ref[pl.ds(i, 256, stride=2), :] = dot(sides[i], down)

    for c in range(4):
        for copy in (to_pair[c], to_chip[c], inc_to_pair[c]):
            copy.wait_send()

        @pl.when(has_up)
        def _():
            to_up[c].wait_send()

        @pl.when(has_down)
        def _():
            to_down[c].wait_send()


def body(
    child_spec,
    interp_theta,
    interp_phi,
    shift_angle,
    trans_op,
    parent_of,
    octant_of,
    sources,
    kinds,
):
    layers = lax.axis_size("wide")
    rows = child_spec.reshape(8, 2, 2, 16, 128).transpose(0, 1, 3, 2, 4).reshape(512, 128)
    angle = shift_angle.reshape(8, 64, 128).transpose(1, 0, 2).reshape(512, 128)
    planes = trans_op.reshape(32, 2, 64, 128).transpose(0, 2, 1, 3).reshape(32, 128, 128)
    quarter = (4, 2, 16, 128)
    vmem = pl.BlockSpec(memory_space=pltpu.VMEM)
    result = pl.pallas_call(
        functools.partial(kernel, layers),
        out_shape=pltpu.VMEM((512, 128), F32),
        in_specs=[pl.BlockSpec(memory_space=pl.ANY)] * 9,
        out_specs=vmem,
        scratch_shapes=[
            pltpu.SMEM((1, 8), jnp.int32),
            pltpu.SMEM((1, 8), jnp.int32),
            pltpu.SMEM((1, 4, 6), jnp.int32),
            pltpu.SMEM((1, 4, 6), jnp.int32),
            pltpu.VMEM((512, 128), BF16),
            pltpu.VMEM((32, 64), BF16),
            pltpu.VMEM((64, 128), BF16),
            pltpu.VMEM((512, 128), F32),
            pltpu.SemaphoreType.DMA((8,)),
            pltpu.VMEM((8, 64, 128), F32),
            pltpu.VMEM((8, 64, 128), F32),
            pltpu.VMEM((8, 256, 128), F32),
            pltpu.VMEM((2, 4) + quarter, BF16),
            pltpu.VMEM((4,) + quarter, BF16),
            pltpu.VMEM((4,) + quarter, BF16),
            pltpu.VMEM((4,) + quarter, BF16),
            pltpu.VMEM((4,) + quarter, BF16),
            pltpu.VMEM((32, 64, 128), F32),
            pltpu.VMEM((32, 2, 32, 128), F32),
            pltpu.VMEM((4,) + quarter, BF16),
            pltpu.VMEM((2, 128, 1024), BF16),
            pltpu.VMEM((2, 256, 256), BF16),
            pltpu.SemaphoreType.DMA,
            pltpu.SemaphoreType.DMA((20,)),
            pltpu.SemaphoreType.DMA((20,)),
        ]
        + [pltpu.VMEM(quarter, BF16)] * 12,
        compiler_params=pltpu.CompilerParams(collective_id=0, has_side_effects=True),
        name="mlfma",
    )(parent_of, octant_of, sources, kinds, rows, interp_theta.T, interp_phi.T, angle, planes)
    result = result.reshape(8, 2, 16, 2, 128).transpose(0, 1, 3, 2, 4)
    return result.reshape(1, 8, 2, 2, 2048)


def solution(mesh):
    placed = (
        P("wide", "narrow", None, None, None),
        P(),
        P(),
        P(),
        P(),
        P("wide", "narrow"),
        P("wide", "narrow"),
        P("wide", None, None),
        P("wide", None, None),
    )
    return jax.shard_map(
        body,
        mesh=mesh,
        in_specs=placed,
        out_specs=P("wide", "narrow", None, None, None),
        check_vma=False,
    )
```

```python
import functools

import jax
import jax.numpy as jnp
from jax import lax
from jax.experimental import pallas as pl
from jax.experimental.pallas import tpu as pltpu
from jax.sharding import PartitionSpec as P

MESH = pl.DeviceIdType.MESH
F32 = jnp.float32
BF16 = jnp.bfloat16


def iota(shape, dim):
    return lax.broadcasted_iota(jnp.int32, shape, dim)


def one_hot(mask):
    return jnp.where(mask, 1.0, 0.0).astype(BF16)


def dot(a, b, dims=((1,), (0,))):
    return lax.dot_general(a, b, (dims, ((), ())), preferred_element_type=F32)


def polar_matrices(theta_t):
    row = iota((64, 32), 0)
    pick_row = one_hot(iota((64, 32), 1) == 2 * (row & 15) + (row >> 5))
    full = dot(pick_row, theta_t)
    full = jnp.concatenate([full, full], axis=1)
    same = (iota((64, 128), 1) >> 6) == ((iota((64, 128), 0) >> 4) & 1)
    down = jnp.where(same, full, 0.0).astype(BF16)
    col = iota((32, 128), 1)
    pick_col = one_hot(iota((32, 128), 0) == 2 * ((col >> 1) & 15) + (col >> 6))
    short = dot(theta_t, pick_col, ((0,), (0,)))
    full = jnp.concatenate([short] * 4, axis=0)
    row, col = iota((256, 128), 0), iota((256, 128), 1)
    same = ((row >> 7) == ((col >> 5) & 1)) & (((row >> 6) & 1) == (col & 1))
    up = jnp.where(same, full, 0.0).astype(BF16)
    return up, down


def azimuth_up(phi_t):
    full = phi_t.astype(F32)
    full = jnp.concatenate([full, full], axis=1)
    full = jnp.concatenate([full, full], axis=0)
    same = (iota((128, 256), 0) >> 6) == (iota((128, 256), 1) >> 7)
    return jnp.where(same, full, 0.0).astype(BF16)


def azimuth_down(phi_t):
    spread = one_hot((iota((64, 128), 1) & 63) == iota((64, 128), 0))
    full = dot(phi_t, spread, ((0,), (0,)))
    full = jnp.concatenate([full, full], axis=0)
    same = (iota((256, 128), 0) >> 7) == (iota((256, 128), 1) >> 6)
    return jnp.where(same, full, 0.0).astype(BF16)


def cos_sin(angle):
    half = 0.5 * angle
    z = half * half
    sine, cosine = 1.0 / 6227020800.0, 1.0 / 479001600.0
    for below_sine, below_cosine in (
        (-1.0 / 39916800.0, -1.0 / 3628800.0),
        (1.0 / 362880.0, 1.0 / 40320.0),
        (-1.0 / 5040.0, -1.0 / 720.0),
        (1.0 / 120.0, 1.0 / 24.0),
        (-1.0 / 6.0, -0.5),
        (1.0, 1.0),
    ):
        sine = sine * z + below_sine
        cosine = cosine * z + below_cosine
    sine = sine * half
    twice = sine + sine
    return 1.0 - twice * sine, twice * cosine


def kernel(
    layers,
    parent_hbm,
    octant_hbm,
    source_hbm,
    kind_hbm,
    spec_hbm,
    theta_hbm,
    phi_hbm,
    angle_hbm,
    trans_hbm,
    out_ref,
    parent_ref,
    octant_ref,
    source_ref,
    kind_ref,
    spec_ref,
    theta_ref,
    phi_ref,
    angle_ref,
    input_sem,
    cos_tab,
    sin_tab,
    fine,
    part,
    pair_in,
    chip_out,
    chip_in,
    own,
    trans_raw,
    trans,
    inc_own,
    back,
    sides,
    load_sem,
    send_sem,
    recv_sem,
    *arrivals,
):
    below, above, inc_pair = arrivals[0:4], arrivals[4:8], arrivals[8:12]
    wide = lax.axis_index("wide")
    narrow = lax.axis_index("narrow")
    chip = narrow // 2
    core = narrow % 2
    odd = wide % 2
    pair_id = {"wide": wide, "narrow": 2 * chip + (1 - core)}
    chip_id = {"wide": wide, "narrow": 2 * (1 - chip) + core}
    up_id = {"wide": lax.rem(wide + 1, layers), "narrow": 2 * ((chip + odd) % 2) + core}
    down_id = {
        "wide": lax.rem(wide + layers - 1, layers),
        "narrow": 2 * ((chip + 1 - odd) % 2) + core,
    }
    has_up = wide < layers - 1
    has_down = wide > 0

    def greet(target):
        pl.semaphore_signal(barrier, inc=1, device_id=target, device_id_type=MESH)

    barrier = pltpu.get_barrier_semaphore()

    @pl.when(has_up)
    def _():
        greet(up_id)

    @pl.when(has_down)
    def _():
        greet(down_id)

    greet(chip_id)
    greet(pair_id)
    inputs = [
        pltpu.make_async_copy(src, dst, input_sem.at[slot])
        for slot, (src, dst) in enumerate(
            (
                (theta_hbm, theta_ref),
                (phi_hbm, phi_ref),
                (spec_hbm, spec_ref),
                (angle_hbm, angle_ref),
                (parent_hbm, parent_ref),
                (octant_hbm, octant_ref),
                (source_hbm, source_ref),
                (kind_hbm, kind_ref),
            )
        )
    ]
    for copy in inputs:
        copy.start()
    load = pltpu.make_async_copy(
        trans_hbm.at[:, pl.ds(pl.multiple_of(core * 64, 64), 64), :], trans_raw, load_sem
    )

    load.start()

    def remote(slot, src, dst, target):
        return pltpu.make_async_remote_copy(
            src_ref=src,
            dst_ref=dst,
            send_sem=send_sem.at[slot],
            recv_sem=recv_sem.at[slot],
            device_id=target,
            device_id_type=MESH,
        )

    home_quarter = 2 * core
    away_quarter = 2 * (1 - core)
    chunks = [(i, g) for i in range(2) for g in range(2)]
    to_pair, to_chip, to_up, to_down, inc_to_pair = [], [], [], [], []
    for c, (i, g) in enumerate(chunks):
        to_pair.append(remote(c, part.at[i, away_quarter + g], pair_in.at[c], pair_id))
        to_chip.append(remote(4 + c, chip_out.at[c], chip_in.at[c], chip_id))
        to_up.append(remote(8 + c, own.at[c], below[c], up_id))
        to_down.append(remote(12 + c, own.at[c], above[c], down_id))
        inc_to_pair.append(remote(16 + c, inc_own.at[c], inc_pair[c], pair_id))

    inputs[0].wait()
    polar_up, polar_down = polar_matrices(theta_ref[...])
    for copy in inputs[1:]:
        copy.wait()
    phi_t = phi_ref[...]
    azimuth = azimuth_up(phi_t)
    for child in range(8):
        coarse = dot(spec_ref[child * 64 : child * 64 + 64, :], azimuth).astype(BF16)
        coarse = jnp.concatenate([coarse[:, 0:128], coarse[:, 128:256]], axis=0)
        fine[child] = dot(polar_up, coarse)
        angle = angle_ref[pl.ds(child, 64, stride=8), :]
        cos_tab[child], sin_tab[child] = cos_sin(angle)

    def partials(i, which):
        rows = pl.ds(pl.multiple_of(which * 16, 16), 16)

        def add(step, sums):
            sums = list(sums)
            for child in (4 * step, 4 * step + 1, 4 * step + 2, 4 * step + 3):
                octant = octant_ref[0, child]
                home = parent_ref[0, child]
                real = fine[child, pl.ds(pl.multiple_of(i * 64 + which * 16, 16), 16), :]
                imag = fine[child, pl.ds(pl.multiple_of(128 + i * 64 + which * 16, 16), 16), :]
                cosine = cos_tab[octant, rows, :]
                sine = sin_tab[octant, rows, :]
                turned_real = real * cosine - imag * sine
                turned_imag = real * sine + imag * cosine
                for parent in range(4):
                    weight = jnp.where(home == parent, 1.0, 0.0)
                    sums[2 * parent] = sums[2 * parent] + weight * turned_real
                    sums[2 * parent + 1] = sums[2 * parent + 1] + weight * turned_imag
            return tuple(sums)

        sums = lax.fori_loop(0, 2, add, tuple(jnp.zeros((16, 128), F32) for _ in range(8)))
        for parent in range(4):
            part[i, which, parent, 0] = sums[2 * parent].astype(BF16)
            part[i, which, parent, 1] = sums[2 * parent + 1].astype(BF16)

    for c, (i, g) in enumerate(chunks):
        partials(i, away_quarter + g)
        if c == 0:
            greeted = 2 + has_up.astype(jnp.int32) + has_down.astype(jnp.int32)
            pl.semaphore_wait(barrier, greeted)
        to_pair[c].start()
    for c, (i, g) in enumerate(chunks):
        partials(i, home_quarter + g)
        to_pair[c].wait_recv()
        chip_out[c] = (part[i, home_quarter + g].astype(F32) + pair_in[c].astype(F32)).astype(BF16)
        to_chip[c].start()

    load.wait()

    def split(kind, carry):
        for t in range(2):
            trans[kind, t] = trans_raw[kind, pl.ds(t, 32, stride=2), :]
        return carry

    lax.fori_loop(0, 32, split, 0)
    down = azimuth_down(phi_t)

    @pl.when(wide == 0)
    def _():
        for ref in below:
            ref[...] = jnp.zeros_like(ref)

    @pl.when(wide == layers - 1)
    def _():
        for ref in above:
            ref[...] = jnp.zeros_like(ref)

    for c in range(4):
        to_chip[c].wait_recv()
        own[c] = (chip_out[c].astype(F32) + chip_in[c].astype(F32)).astype(BF16)

        @pl.when(has_up)
        def _():
            to_up[c].start()

        @pl.when(has_down)
        def _():
            to_down[c].start()

    for c, (i, g) in enumerate(chunks):

        @pl.when(has_down)
        def _():
            to_up[c].wait_recv()

        @pl.when(has_up)
        def _():
            to_down[c].wait_recv()

        pools = (below[c], below[c], own.at[c], own.at[c], above[c], above[c])
        for parent in range(4):
            real_sum = jnp.zeros((16, 128), F32)
            imag_sum = jnp.zeros((16, 128), F32)
            for column, pool in enumerate(pools):
                source = lax.rem(source_ref[0, parent, column], 4)
                kind = kind_ref[0, parent, column]
                table_real = trans[kind, 0, g * 16 : g * 16 + 16, :]
                table_imag = trans[kind, 1, g * 16 : g * 16 + 16, :]
                real = pool[source, 0].astype(F32)
                imag = pool[source, 1].astype(F32)
                real_sum = real_sum + table_real * real - table_imag * imag
                imag_sum = imag_sum + table_real * imag + table_imag * real
            inc_own[c, parent, 0] = real_sum.astype(BF16)
            inc_own[c, parent, 1] = imag_sum.astype(BF16)
        inc_to_pair[c].start()

    def turn_back(i, values, which):
        rows = pl.ds(pl.multiple_of(which * 16, 16), 16)

        def one(step, carry):
            for child in (4 * step, 4 * step + 1, 4 * step + 2, 4 * step + 3):
                home = parent_ref[0, child]
                octant = octant_ref[0, child]
                cosine = cos_tab[octant, rows, :]
                sine = sin_tab[octant, rows, :]
                real = values[home, 0].astype(F32)
                imag = values[home, 1].astype(F32)
                lanes = pl.ds(pl.multiple_of(child * 128, 128), 128)
                back[i, pl.ds(pl.multiple_of(which * 16, 16), 16), lanes] = (
                    real * cosine + imag * sine
                ).astype(BF16)
                back[i, pl.ds(pl.multiple_of(64 + which * 16, 16), 16), lanes] = (
                    imag * cosine - real * sine
                ).astype(BF16)
            return carry

        lax.fori_loop(0, 2, one, 0)

    for c, (i, g) in enumerate(chunks):
        turn_back(i, inc_own.at[c], home_quarter + g)

    for i in range(2):
        for g in range(2):
            inc_to_pair[2 * i + g].wait_recv()
            turn_back(i, inc_pair[2 * i + g], away_quarter + g)
        lowered = dot(polar_down, back[i]).astype(BF16)
        for child in range(8):
            for e in range(2):
                sides[i, child * 32 : child * 32 + 32, e * 128 : e * 128 + 128] = lowered[
                    e * 32 : e * 32 + 32, child * 128 : child * 128 + 128
                ]
        out_ref[pl.ds(i, 256, stride=2), :] = dot(sides[i], down)

    for c in range(4):
        for copy in (to_pair[c], to_chip[c], inc_to_pair[c]):
            copy.wait_send()

        @pl.when(has_up)
        def _():
            to_up[c].wait_send()

        @pl.when(has_down)
        def _():
            to_down[c].wait_send()


def body(
    child_spec,
    interp_theta,
    interp_phi,
    shift_angle,
    trans_op,
    parent_of,
    octant_of,
    sources,
    kinds,
):
    layers = lax.axis_size("wide")
    rows = child_spec.reshape(8, 2, 2, 16, 128).transpose(0, 1, 3, 2, 4).reshape(512, 128)
    angle = shift_angle.reshape(8, 64, 128).transpose(1, 0, 2).reshape(512, 128)
    planes = trans_op.reshape(32, 2, 64, 128).transpose(0, 2, 1, 3).reshape(32, 128, 128)
    quarter = (4, 2, 16, 128)
    vmem = pl.BlockSpec(memory_space=pltpu.VMEM)
    result = pl.pallas_call(
        functools.partial(kernel, layers),
        out_shape=pltpu.VMEM((512, 128), F32),
        in_specs=[pl.BlockSpec(memory_space=pl.ANY)] * 9,
        out_specs=vmem,
        scratch_shapes=[
            pltpu.SMEM((1, 8), jnp.int32),
            pltpu.SMEM((1, 8), jnp.int32),
            pltpu.SMEM((1, 4, 6), jnp.int32),
            pltpu.SMEM((1, 4, 6), jnp.int32),
            pltpu.VMEM((512, 128), BF16),
            pltpu.VMEM((32, 64), BF16),
            pltpu.VMEM((64, 128), BF16),
            pltpu.VMEM((512, 128), F32),
            pltpu.SemaphoreType.DMA((8,)),
            pltpu.VMEM((8, 64, 128), F32),
            pltpu.VMEM((8, 64, 128), F32),
            pltpu.VMEM((8, 256, 128), F32),
            pltpu.VMEM((2, 4) + quarter, BF16),
            pltpu.VMEM((4,) + quarter, BF16),
            pltpu.VMEM((4,) + quarter, BF16),
            pltpu.VMEM((4,) + quarter, BF16),
            pltpu.VMEM((4,) + quarter, BF16),
            pltpu.VMEM((32, 64, 128), F32),
            pltpu.VMEM((32, 2, 32, 128), F32),
            pltpu.VMEM((4,) + quarter, BF16),
            pltpu.VMEM((2, 128, 1024), BF16),
            pltpu.VMEM((2, 256, 256), BF16),
            pltpu.SemaphoreType.DMA,
            pltpu.SemaphoreType.DMA((20,)),
            pltpu.SemaphoreType.DMA((20,)),
        ]
        + [pltpu.VMEM(quarter, BF16)] * 12,
        compiler_params=pltpu.CompilerParams(collective_id=0, has_side_effects=True),
        name="mlfma",
    )(parent_of, octant_of, sources, kinds, rows, interp_theta.T, interp_phi.T, angle, planes)
    result = result.reshape(8, 2, 16, 2, 128).transpose(0, 1, 3, 2, 4)
    return result.reshape(1, 8, 2, 2, 2048)


def solution(mesh):
    placed = (
        P("wide", "narrow", None, None, None),
        P(),
        P(),
        P(),
        P(),
        P("wide", "narrow"),
        P("wide", "narrow"),
        P("wide", None, None),
        P("wide", None, None),
    )
    return jax.shard_map(
        body,
        mesh=mesh,
        in_specs=placed,
        out_specs=P("wide", "narrow", None, None, None),
        check_vma=False,
    )
```
